32 devices in a mesh: seq: 4 (over y, x), chan: 8 (over z, core).
Axes of the slice: x: 2, y: 2, z: 4, core: 2. Of those that a mesh axis runs over, the one named last changes fastest.
Arguments:
- query_stream: bfloat16 [2048, 8192], P('seq', 'chan'), may hold values from -6 to 6
- key_stream: bfloat16 [2048, 8192], P('seq', 'chan'), may hold values from -6 to 6
- value_stream: bfloat16 [2048, 8192], P('seq', 'chan'), may hold values from -6 to 6
- teacher_filter: float32 [512, 128], P('chan'), may hold values from -0.5 to 0.5
- student_filter: float32 [512, 128], P('chan'), may hold values from -0.5 to 0.5
- group_mask: int32 [512], P('chan'), may hold values 0 or 1
- base_ids: int32 [2048], replicated, may hold values from 0 to 7
- teacher_proj: bfloat16 [8192, 8192], P('chan', 'seq'), may hold values from -0.0625 to 0.0625
- student_proj: bfloat16 [8192, 8192], P('chan', 'seq'), may hold values from -0.09375 to 0.09375
Outputs:
- proj_grad: float32 [8192, 8192], P('chan', 'seq')
The draws below stay inside these ranges and needn't reach their ends.
All inputs are finite; a program needn't handle non-finite values. No bound on the sum of `group_mask` on one device may be relied on, other than what follows from the above.
Results may differ from the reference program's by a relative error of at most 0.022.
Values may be sent and summed in bfloat16 or wider, within the bound.
A program may use at most 128 MiB of HBM per device.

```python
import jax
import jax.numpy as jnp
from jax import lax

D = 8192
KERNEL = 128
GROUP_CH = 16
TOK_DEV = 512
TOKENS = 2048
GROUPS = 512
N_SEQ = 4
N_CHAN = 8


def with_ends(result, rng, low, largest):
    shape = result.shape
    spot = [jax.random.randint(jax.random.fold_in(rng, axis), (), 0, shape[axis]) for axis in range(len(shape))]
    result = result.at[tuple(spot)].set(low)
    longest = shape.index(max(shape))
    spot[longest] = (spot[longest] + 1) % shape[longest]
    return result.at[tuple(spot)].set(largest)


def with_spikes(entries, rng, source, target, shards_of, factor):
    def block_of(axis_at):
        return (jnp.arange(entries.shape[axis_at]) // (entries.shape[axis_at] // shards_of)).reshape((-1,) + (1,) * (entries.ndim - 1 - axis_at))

    near = jax.random.permutation(rng, shards_of)[block_of(target)]
    far = (block_of(target) + shards_of // 2) % shards_of
    return jnp.where((block_of(source) == near) | (block_of(source) == far), factor * entries, entries)


def block_levels(own_key, dims, shards, low, high):
    loudness = 1.0
    for position, shards_of in shards:
        draws = jax.random.uniform(jax.random.fold_in(jax.random.fold_in(own_key, 6), position), (shards_of,), jnp.float32, low / len(shards), high / len(shards))
        loudness = loudness * jnp.repeat(jnp.exp(draws), dims[position] // shards_of).reshape((-1,) + (1,) * (len(dims) - 1 - position))
    return loudness


def centred(rng, dims, deviation, limit, split=(), kind=jnp.bfloat16):
    drawn = jax.random.normal(rng, dims, jnp.float32) * deviation
    if len(split) > 0:
        drawn = block_levels(rng, dims, split, -0.22, 0.18) * drawn
    return jnp.clip(drawn, min=-limit, max=limit).astype(kind)


def heavy_noise(own_key, extent, deviation, bound, split, heavy, dtype=jnp.bfloat16):
    result = deviation * jax.random.normal(own_key, extent, jnp.float32)
    if split:
        result = result * block_levels(own_key, extent, split, -0.22, 0.18)
    return jnp.clip(with_spikes(result, jax.random.fold_in(own_key, 3), *heavy), -bound, bound).astype(dtype)


def setup_inputs(seed: int = 0) -> dict:
    arg_keys = jax.random.split(jax.random.key(seed), 10)
    query_stream = centred(arg_keys[0], (TOKENS, D), 1.0, 6.0, ((0, 4), (1, 8)))
    key_stream = centred(arg_keys[1], (TOKENS, D), 1.0, 6.0, ((0, 4), (1, 8)))
    value_stream = centred(arg_keys[2], (TOKENS, D), 1.0, 6.0, ((0, 4), (1, 8)))
    teacher_filter = centred(arg_keys[3], (GROUPS, KERNEL), 0.0884, 0.5, ((0, 8),), jnp.float32)
    student_filter = centred(arg_keys[4], (GROUPS, KERNEL), 0.0884, 0.5, ((0, 8),), jnp.float32)
    group_mask = with_ends((jax.random.randint(arg_keys[5], (GROUPS,), 0, 4) < 3).astype(jnp.int32), jax.random.fold_in(arg_keys[5], 1), 0, 1)
    base_ids = with_ends(jax.random.randint(arg_keys[6], (TOKENS,), 0, 8), jax.random.fold_in(arg_keys[6], 1), 0, 7).astype(jnp.int32)
    teacher_proj = centred(arg_keys[7], (D, D), D ** -0.5, 0.0625, ((0, 8), (1, 4)))
    student_proj = heavy_noise(arg_keys[8], (D, D), D ** -0.5, 0.09375, ((0, 8), (1, 4)), (0, 1, 8, 2.0))
    return dict(query_stream=query_stream, key_stream=key_stream, value_stream=value_stream, teacher_filter=teacher_filter, student_filter=student_filter, group_mask=group_mask, base_ids=base_ids, teacher_proj=teacher_proj, student_proj=student_proj)


repeat_weight = 0.1


def filter_stream(stream, filters):
    token_total = stream.shape[0]
    per_channel = jnp.repeat(filters, GROUP_CH, axis=0)
    padded = jnp.concatenate([jnp.zeros((KERNEL - 1, stream.shape[1]), jnp.float32), stream], axis=0)

    def add_tap(tap_index, accumulated):
        shifted = lax.dynamic_slice_in_dim(padded, KERNEL - 1 - tap_index, token_total, 0)
        column = lax.dynamic_slice_in_dim(per_channel, tap_index, 1, 1)[:, 0]
        return accumulated + shifted * column[None, :]

    return lax.fori_loop(0, KERNEL, add_tap, jnp.zeros(stream.shape, jnp.float32))


def reference(query_stream, key_stream, value_stream, teacher_filter, student_filter, group_mask, base_ids, teacher_proj, student_proj):
    gated = (key_stream.astype(jnp.float32) * value_stream.astype(jnp.float32)).astype(jnp.bfloat16)
    gated_wide = lax.optimization_barrier(gated).astype(jnp.float32)
    teacher_mix = filter_stream(gated_wide, teacher_filter)
    student_mix = filter_stream(gated_wide, student_filter)
    keep = jnp.repeat(group_mask.astype(jnp.float32), GROUP_CH)
    queries = query_stream.astype(jnp.float32)
    teacher_out = (queries * teacher_mix).astype(jnp.bfloat16)
    student_out = (queries * student_mix * keep[None, :]).astype(jnp.bfloat16)
    block_width = D // N_CHAN

    def add_block(block, accumulated):
        student_part = lax.dynamic_slice_in_dim(student_out, block * block_width, block_width, 1)
        teacher_part = lax.dynamic_slice_in_dim(teacher_out, block * block_width, block_width, 1)
        student_rows = lax.dynamic_slice_in_dim(student_proj, block * block_width, block_width, 0)
        teacher_rows = lax.dynamic_slice_in_dim(teacher_proj, block * block_width, block_width, 0)
        part = jnp.dot(student_part, student_rows, preferred_element_type=jnp.float32) - jnp.dot(teacher_part, teacher_rows, preferred_element_type=jnp.float32)
        return accumulated + lax.optimization_barrier(part.astype(jnp.bfloat16)).astype(jnp.float32)

    summed = lax.fori_loop(0, N_CHAN, add_block, jnp.zeros((TOKENS, D), jnp.float32))
    residual = lax.optimization_barrier(summed.astype(jnp.bfloat16)).astype(jnp.float32)
    scale = float(TOKENS) ** -0.5
    token_weight = jnp.where(base_ids >= 4, repeat_weight, 1.0).astype(jnp.float32) * scale
    adjoint = (residual * token_weight[:, None]).astype(jnp.bfloat16)

    def add_rows(block, accumulated):
        student_rows = lax.dynamic_slice_in_dim(student_out, block * TOK_DEV, TOK_DEV, 0)
        adjoint_rows = lax.dynamic_slice_in_dim(adjoint, block * TOK_DEV, TOK_DEV, 0)
        part = jnp.dot(student_rows.T, adjoint_rows, preferred_element_type=jnp.float32)
        return accumulated + lax.optimization_barrier(part.astype(jnp.bfloat16)).astype(jnp.float32)

    return lax.fori_loop(0, N_SEQ, add_rows, jnp.zeros((D, D), jnp.float32))
```

```python
import functools

import jax
import jax.numpy as jnp
from jax import lax
from jax.experimental import pallas as pl
from jax.experimental.pallas import tpu as pltpu
from jax.sharding import PartitionSpec as P

repeat_weight = 0.1
lanes = 128
widest_cut = 512
depth = 16
pair_lag = 2
edge_lag = 5
exchange_lag = 3
up_lag = 3
share_lag = 2
vmem_limit = 66_000_000


def flipped(position, bits):
    result = position
    step = 1
    while step <= bits:
        if bits & step:
            result = result + step - 2 * step * ((position // step) % 2)
        step *= 2
    return result


def chan_bit(position, bit):
    return (position // (1 << bit)) % 2


def exchange_flips(chan_count):
    bits = chan_count.bit_length() - 1
    assert bits >= 3 and chan_count == 1 << bits
    return [6] + [1 << bit for bit in range(3, bits)]


def own_order(blocks):
    late = blocks // 2
    return list(range(late, blocks)) + list(range(late - 1, -1, -1))


def slot_order(seq_count, blocks):
    assert seq_count >= 4
    own = own_order(blocks)
    order = [(0, block) for block in own]
    for block in own:
        order += [(1, block), (2, block)]
    for k in range(3, seq_count):
        order += [(k, block) for block in own]
    return order


def fused_kernel(
    seq_count,
    chan_count,
    width,
    scale,
    query_hbm,
    key_hbm,
    value_hbm,
    teacher_taps,
    student_taps,
    mask_ref,
    ids_ref,
    teacher_hbm,
    student_hbm,
    total_ref,
    query,
    key,
    value,
    gated,
    base,
    tables,
    weights,
    mixes,
    teacher_w,
    student_w,
    part,
    hold,
    adjoint,
    transposed,
    pair_in,
    edge_in,
    middle_in,
    local_sem,
    halo_sem,
    seq_send,
    seq_recv,
    pair_send,
    pair_recv,
    edge_send,
    edge_recv,
    middle_send,
    middle_recv,
    up_send,
    up_recv,
    share_send,
    share_recv,
):
    tokens, channels = query.shape
    taps = teacher_taps.shape[1]
    groups = teacher_taps.shape[0]
    blocks = tokens // taps
    columns = teacher_w.shape[1]
    cut = part.shape[2]
    cuts = columns // cut
    half = taps // 2
    own = own_order(blocks)
    order = slot_order(seq_count, blocks)
    items = len(order) * cuts
    flips = exchange_flips(chan_count)
    per_chunk = lanes // width
    chunks = channels // lanes
    seq_me = lax.axis_index("seq")
    chan_me = lax.axis_index("chan")
    inner = chan_bit(chan_me, 1) != chan_bit(chan_me, 2)
    mine = chan_bit(chan_me, 0) * half
    others = half - mine

    local = [
        pltpu.make_async_copy(source, target, local_sem.at[index])
        for index, (source, target) in enumerate(
            [
                (key_hbm, key),
                (value_hbm, value),
                (query_hbm, query),
                (teacher_hbm, teacher_w),
                (student_hbm, student_w),
            ]
        )
    ]
    for copy in local:
        copy.start()

    def along_chan(bits):
        return {"seq": seq_me, "chan": flipped(chan_me, bits)}

    pair_partner = along_chan(1)
    edge_partner = along_chan(2)
    middle_partners = [along_chan(bits) for bits in flips]
    seq_partners = [{"seq": flipped(seq_me, k), "chan": chan_me} for k in range(1, seq_count)]
    everyone = [pair_partner, edge_partner] + middle_partners + seq_partners
    barrier = pltpu.get_barrier_semaphore()
    for partner in everyone:
        pl.semaphore_signal(
            barrier, inc=1, device_id=partner, device_id_type=pl.DeviceIdType.MESH
        )

    def remote(source, target, send_sem, recv_sem, partner):
        return pltpu.make_async_remote_copy(
            src_ref=source,
            dst_ref=target,
            send_sem=send_sem,
            recv_sem=recv_sem,
            device_id=partner,
            device_id_type=pl.DeviceIdType.MESH,
        )

    row = lax.broadcasted_iota(jnp.int32, (taps, 2 * taps), 0)
    column = lax.broadcasted_iota(jnp.int32, (taps, 2 * taps), 1)
    reverse = jnp.where(row + column == taps, 1.0, 0.0).astype(jnp.bfloat16)
    row = lax.broadcasted_iota(jnp.int32, (groups, groups), 0)
    column = lax.broadcasted_iota(jnp.int32, (groups, groups), 1)
    keep = jnp.broadcast_to(mask_ref[...].astype(jnp.float32), (groups, groups))
    keep = jnp.where(row == column, keep, 0.0).astype(jnp.bfloat16)
    kept = jnp.dot(
        keep, student_taps[...].astype(jnp.bfloat16), preferred_element_type=jnp.float32
    )
    base[0] = -jnp.dot(
        teacher_taps[...].astype(jnp.bfloat16), reverse, preferred_element_type=jnp.float32
    )
    base[1] = jnp.dot(kept.astype(jnp.bfloat16), reverse, preferred_element_type=jnp.float32)

    for slot, (k, block) in enumerate(order):
        ids = ids_ref[pl.ds(flipped(seq_me, k) * blocks + block, 1), :]
        weights[slot : slot + 1, :] = jnp.where(ids >= 4, repeat_weight, 1.0) * scale

    local[0].wait()
    local[1].wait()
    gated[taps:, :] = (key[...].astype(jnp.float32) * value[...].astype(jnp.float32)).astype(
        jnp.bfloat16
    )

    @pl.when(seq_me == 0)
    def _():
        gated[0:taps, :] = jnp.zeros((taps, channels), jnp.bfloat16)

    pl.semaphore_wait(barrier, len(everyone))

    def halo(target_seq):
        return remote(
            gated.at[pl.ds(tokens, taps)],
            gated.at[pl.ds(0, taps)],
            halo_sem.at[0],
            halo_sem.at[1],
            {"seq": target_seq, "chan": chan_me},
        )

    @pl.when(seq_me + 1 < seq_count)
    def _():
        halo(seq_me + 1).start()

    local[2].wait()

    def mix_chunk(chunk, which, build):
        span = pl.ds(pl.multiple_of(chunk * lanes, lanes), lanes)
        windows = jnp.concatenate(
            [gated[block * taps : (block + 2) * taps, span] for block in which], axis=1
        )
        lane_group = (
            lax.broadcasted_iota(jnp.int32, (2 * taps, len(which) * lanes), 1) % lanes // width
        )
        rows = [base[kind, pl.ds(chunk * per_chunk, per_chunk), :] for kind in range(2)]
        mixed = None
        for group in range(per_chunk):
            place = chunk * per_chunk + group
            if build:
                table = jnp.concatenate(
                    [
                        pltpu.roll(
                            jnp.broadcast_to(
                                rows[kind][group : group + 1, :], (taps, 2 * taps)
                            ),
                            0,
                            1,
                            stride=1,
                            stride_axis=0,
                        ).astype(jnp.bfloat16)
                        for kind in range(2)
                    ],
                    axis=0,
                )
                tables[place] = table
            else:
                table = tables[place]
            product = jnp.dot(table, windows, preferred_element_type=jnp.float32)
            mixed = product if mixed is None else jnp.where(lane_group == group, product, mixed)
        for index, block in enumerate(which):
            slot = order.index((0, block))
            queries = query[block * taps : (block + 1) * taps, span].astype(jnp.float32)
            for kind in range(2):
                mixes[slot, kind, :, span] = (
                    queries
                    * mixed[
                        kind * taps : (kind + 1) * taps, index * lanes : (index + 1) * lanes
                    ]
                ).astype(jnp.bfloat16)

    def seq_copy(source, target, partner):
        return remote(
            mixes.at[source], mixes.at[target], seq_send.at[target], seq_recv.at[target], partner
        )

    def send_block(block):
        source = order.index((0, block))
        for k in range(1, seq_count):
            if k != 3:
                seq_copy(source, order.index((k, block)), seq_partners[k - 1]).start()

    early = blocks - blocks // 2

    @pl.loop(0, chunks)
    def _(chunk):
        mix_chunk(chunk, own[:early], True)

    for block in own[:early]:
        send_block(block)
    local[3].wait()
    local[4].wait()

    def ring(item):
        return lax.rem(item, depth)

    def slab(offset):
        return pl.ds(pl.multiple_of(offset, 16), half)

    def pair_down(item):
        return remote(
            part.at[ring(item), slab(others)],
            pair_in.at[item],
            pair_send.at[ring(item)],
            pair_recv.at[item],
            pair_partner,
        )

    def edge_down(item):
        return remote(
            part.at[ring(item), slab(mine)],
            edge_in.at[item],
            edge_send.at[ring(item)],
            edge_recv.at[item],
            edge_partner,
        )

    def middle(index, item):
        source = part.at[ring(item), slab(mine)]
        if index > 0:
            source = hold.at[index - 1, ring(item)]
        return remote(
            source,
            middle_in.at[index, item],
            middle_send.at[index, ring(item)],
            middle_recv.at[index, item],
            middle_partners[index],
        )

    def edge_up(item):
        place = adjoint.at[item, slab(mine)]
        return remote(place, place, up_send.at[ring(item)], up_recv.at[item], edge_partner)

    def share(item, incoming=False):
        place = adjoint.at[item, slab(others if incoming else mine)]
        return remote(
            place, place, share_send.at[ring(item)], share_recv.at[item], pair_partner
        )

    def multiply(item):
        slot = item // cuts
        span = pl.ds(pl.multiple_of(item % cuts * cut, cut), cut)

        @pl.when(jnp.logical_and(slot >= blocks, item % cuts == 0))
        def _():
            seq_copy(slot, slot, seq_partners[0]).wait_recv()

        for index, block in enumerate(own):
            near = 1 + index % 2
            source = order.index((near, block))

            @pl.when(item == source * cuts)
            def _():
                seq_copy(source, order.index((3, block)), seq_partners[2 - near]).start()

        @pl.when(item >= depth)
        def _():
            pair_down(item - depth).wait_send()

            @pl.when(inner)
            def _():
                middle(0, item - depth).wait_send()

            @pl.when(jnp.logical_not(inner))
            def _():
                edge_down(item - depth).wait_send()

        student = jnp.dot(mixes[slot, 1], student_w[:, span], preferred_element_type=jnp.float32)
        teacher = jnp.dot(mixes[slot, 0], teacher_w[:, span], preferred_element_type=jnp.float32)
        part[ring(item)] = (student + teacher).astype(jnp.bfloat16)
        pair_down(item).start()

    def held(item):
        return part[ring(item), slab(mine)].astype(jnp.float32)

    def fold_edge(item):
        pair_down(item).wait_recv()
        part[ring(item), slab(mine)] = (held(item) + pair_in[item].astype(jnp.float32)).astype(
            jnp.bfloat16
        )
        edge_down(item).start()

    def fold_inner(item):
        pair_down(item).wait_recv()
        edge_down(item).wait_recv()
        part[ring(item), slab(mine)] = (
            held(item) + pair_in[item].astype(jnp.float32) + edge_in[item].astype(jnp.float32)
        ).astype(jnp.bfloat16)
        middle(0, item).start()

    def exchange(index, item):
        middle(index, item).wait_recv()
        if index > 0:
            total = hold[index - 1, ring(item)].astype(jnp.float32)
        else:
            total = held(item)
        total = (total + middle_in[index, item].astype(jnp.float32)).astype(jnp.bfloat16)
        if index + 1 < len(flips):

            @pl.when(item >= depth)
            def _():
                middle(index + 1, item - depth).wait_send()

            hold[index, ring(item)] = total
            middle(index + 1, item).start()
        else:

            @pl.when(item >= depth)
            def _():
                edge_up(item - depth).wait_send()
                share(item - depth).wait_send()

            adjoint[item, slab(mine)] = total
            edge_up(item).start()
            share(item).start()

    def spread_edge(item):
        edge_up(item).wait_recv()

        @pl.when(item >= depth)
        def _():
            share(item - depth).wait_send()

        share(item).start()

    def accumulate(item):
        slot = item // cuts
        span = pl.ds(pl.multiple_of(item % cuts * cut, cut), cut)
        share(item, True).wait_recv()

        @pl.when(item % cuts == 0)
        def _():
            turned = mixes[slot, 1].T.astype(jnp.float32)
            transposed[...] = (turned * weights[pl.ds(slot, 1), :]).astype(jnp.bfloat16)

        def product():
            return jnp.dot(
                transposed[...], adjoint[item], preferred_element_type=jnp.float32
            )

        @pl.when(slot == 0)
        def _():
            total_ref[:, span] = product()

        @pl.when(slot > 0)
        def _():
            total_ref[:, span] += product()

    per_step = max(1, chunks // cuts)
    late_steps = chunks // per_step
    first_late = early * cuts - late_steps
    assert first_late >= 0

    def mix_late(step):
        @pl.when(step == first_late)
        def _():
            @pl.when(seq_me > 0)
            def _():
                halo(seq_me).wait_recv()

        @pl.when(jnp.logical_and(step >= first_late, step < first_late + late_steps))
        def _():
            @pl.loop(0, per_step)
            def _(index):
                mix_chunk((step - first_late) * per_step + index, own[early:], False)

        @pl.when(step == first_late + late_steps - 1)
        def _():
            for block in own[early:]:
                send_block(block)

    last_lag = edge_lag + exchange_lag * len(flips)
    is_edge = jnp.logical_not(inner)
    stages = [
        (functools.partial(exchange, index), edge_lag + exchange_lag * (index + 1), inner)
        for index in range(len(flips) - 1, -1, -1)
    ]
    stages += [
        (spread_edge, last_lag + up_lag, is_edge),
        (fold_inner, edge_lag, inner),
        (fold_edge, pair_lag, is_edge),
        (multiply, 0, None),
        (
            accumulate,
            last_lag + share_lag + jnp.where(inner, 0, up_lag),
            None,
        ),
    ]

    @pl.loop(0, items + last_lag + up_lag + share_lag)
    def _(step):
        for stage, lag, role in stages:
            item = step - lag
            active = jnp.logical_and(item >= 0, item < items)
            if role is not None:
                active = jnp.logical_and(active, role)

            @pl.when(active)
            def _():
                stage(item)

            if stage is multiply:
                mix_late(step)

    @pl.when(seq_me + 1 < seq_count)
    def _():
        halo(seq_me + 1).wait_send()

    for slot in range(blocks, len(order)):
        seq_copy(slot, slot, seq_partners[0]).wait_send()

    @pl.loop(items - depth, items)
    def _(item):
        pair_down(item).wait_send()
        share(item).wait_send()

        @pl.when(inner)
        def _():
            for index in range(len(flips)):
                middle(index, item).wait_send()
            edge_up(item).wait_send()

        @pl.when(jnp.logical_not(inner))
        def _():
            edge_down(item).wait_send()


def body(
    query_stream,
    key_stream,
    value_stream,
    teacher_filter,
    student_filter,
    group_mask,
    base_ids,
    teacher_proj,
    student_proj,
):
    tokens, channels = query_stream.shape
    groups, taps = teacher_filter.shape
    width = channels // groups
    seq_count = lax.axis_size("seq")
    chan_count = lax.axis_size("chan")
    columns = teacher_proj.shape[1]
    scale = float(tokens * seq_count) ** (-0.5)
    slots = len(slot_order(seq_count, tokens // taps))
    cut = min(widest_cut, columns)
    items = slots * (columns // cut)
    flips = len(exchange_flips(chan_count))
    half = taps // 2

    any_spec = pl.BlockSpec(memory_space=pl.ANY)
    vmem_spec = pl.BlockSpec(memory_space=pltpu.VMEM)
    dma = pltpu.SemaphoreType.DMA
    bf16 = jnp.bfloat16
    return pl.pallas_call(
        functools.partial(fused_kernel, seq_count, chan_count, width, scale),
        out_shape=jax.ShapeDtypeStruct((channels, columns), jnp.float32),
        in_specs=[any_spec] * 3 + [vmem_spec] * 4 + [any_spec] * 2,
        out_specs=vmem_spec,
        scratch_shapes=[
            pltpu.VMEM((tokens, channels), bf16),
            pltpu.VMEM((tokens, channels), bf16),
            pltpu.VMEM((tokens, channels), bf16),
            pltpu.VMEM((taps + tokens, channels), bf16),
            pltpu.VMEM((2, groups, 2 * taps), jnp.float32),
            pltpu.VMEM((groups, 2 * taps, 2 * taps), bf16),
            pltpu.VMEM((slots, taps), jnp.float32),
            pltpu.VMEM((slots, 2, taps, channels), bf16),
            pltpu.VMEM(teacher_proj.shape, bf16),
            pltpu.VMEM(student_proj.shape, bf16),
            pltpu.VMEM((depth, taps, cut), bf16),
            pltpu.VMEM((max(1, flips - 1), depth, half, cut), bf16),
            pltpu.VMEM((items, taps, cut), bf16),
            pltpu.VMEM((channels, taps), bf16),
            pltpu.VMEM((items, half, cut), bf16),
            pltpu.VMEM((items, half, cut), bf16),
            pltpu.VMEM((flips, items, half, cut), bf16),
            dma((5,)),
            dma((2,)),
            dma((slots,)),
            dma((slots,)),
            dma((depth,)),
            dma((items,)),
            dma((depth,)),
            dma((items,)),
            dma((flips, depth)),
            dma((flips, items)),
            dma((depth,)),
            dma((items,)),
            dma((depth,)),
            dma((items,)),
        ],
        compiler_params=pltpu.CompilerParams(
            collective_id=0, has_side_effects=True, vmem_limit_bytes=vmem_limit
        ),
        name="fused",
    )(
        query_stream,
        key_stream,
        value_stream,
        teacher_filter,
        student_filter,
        group_mask[None, :],
        base_ids.reshape(-1, taps),
        teacher_proj,
        student_proj,
    )


def solution(mesh):
    placed = (
        P("seq", "chan"),
        P("seq", "chan"),
        P("seq", "chan"),
        P("chan", None),
        P("chan", None),
        P("chan"),
        P(),
        P("chan", "seq"),
        P("chan", "seq"),
    )
    return jax.shard_map(
        body, mesh=mesh, in_specs=placed, out_specs=P("chan", "seq"), check_vma=False
    )
```

```python
import functools

import jax
import jax.numpy as jnp
from jax import lax
from jax.experimental import pallas as pl
from jax.experimental.pallas import tpu as pltpu
from jax.sharding import PartitionSpec as P

repeat_weight = 0.1
lanes = 128
widest_cut = 512
parts = 1
depth = 16
pair_lag = 1
edge_lag = 4
exchange_lag = 3
up_lag = 3
share_lag = 2
vmem_limit = 57_000_000


def flipped(position, bits):
    result = position
    step = 1
    while step <= bits:
        if bits & step:
            result = result + step - 2 * step * ((position // step) % 2)
        step *= 2
    return result


def chan_bit(position, bit):
    return (position // (1 << bit)) % 2


def exchange_flips(chan_count):
    bits = chan_count.bit_length() - 1
    assert bits >= 3 and chan_count == 1 << bits
    return [6] + [1 << bit for bit in range(3, bits)]


def own_order(blocks):
    late = blocks // 2
    return list(range(late, blocks)) + list(range(late - 1, -1, -1))


def slot_order(seq_count, blocks):
    assert seq_count >= 4
    own = own_order(blocks)
    order = [(0, block) for block in own]
    for block in own:
        order += [(1, block), (2, block)]
    for k in range(3, seq_count):
        order += [(k, block) for block in own]
    return order


def fused_kernel(
    seq_count,
    chan_count,
    width,
    scale,
    query_hbm,
    key_hbm,
    value_hbm,
    teacher_taps,
    student_taps,
    mask_ref,
    ids_ref,
    teacher_hbm,
    student_hbm,
    total_ref,
    query,
    key,
    value,
    gated,
    base,
    tables,
    weights,
    mixes,
    teacher_w,
    student_w,
    part,
    hold,
    adjoint,
    transposed,
    pair_in,
    edge_in,
    middle_in,
    local_sem,
    halo_sem,
    seq_send,
    seq_recv,
    pair_send,
    pair_recv,
    edge_send,
    edge_recv,
    middle_send,
    middle_recv,
    up_send,
    up_recv,
    share_send,
    share_recv,
):
    tokens, channels = query.shape
    taps = teacher_taps.shape[1]
    groups = teacher_taps.shape[0]
    blocks = tokens // taps
    columns = teacher_w.shape[1]
    cut = part.shape[2]
    cuts = columns // cut
    half = taps // 2
    own = own_order(blocks)
    order = slot_order(seq_count, blocks)
    items = len(order) * cuts
    flips = exchange_flips(chan_count)
    per_chunk = lanes // width
    chunks = channels // lanes
    seq_me = lax.axis_index("seq")
    chan_me = lax.axis_index("chan")
    inner = chan_bit(chan_me, 1) != chan_bit(chan_me, 2)
    mine = chan_bit(chan_me, 0) * half
    others = half - mine

    def along_chan(bits):
        return {"seq": seq_me, "chan": flipped(chan_me, bits)}

    pair_partner = along_chan(1)
    edge_partner = along_chan(2)
    middle_partners = [along_chan(bits) for bits in flips]
    seq_partners = [{"seq": flipped(seq_me, k), "chan": chan_me} for k in range(1, seq_count)]
    barrier = pltpu.get_barrier_semaphore()

    def greet(partner):
        pl.semaphore_signal(
            barrier, inc=1, device_id=partner, device_id_type=pl.DeviceIdType.MESH
        )

    always = [pair_partner, edge_partner]
    always += [seq_partners[k - 1] for k in range(1, seq_count) if k != 3]
    across = jnp.logical_or(seq_me % 4 == 1, seq_me % 4 == 2)

    @pl.when(across)
    def _():
        greet(seq_partners[2])

    for partner in always:
        greet(partner)

    @pl.when(inner)
    def _():
        for partner in middle_partners:
            greet(partner)

    local = [
        pltpu.make_async_copy(source, target, local_sem.at[index])
        for index, (source, target) in enumerate(
            [
                (key_hbm, key),
                (value_hbm, value),
                (query_hbm, query),
                (teacher_hbm, teacher_w),
                (student_hbm, student_w),
            ]
        )
    ]
    for copy in local:
        copy.start()

    def remote(source, target, send_sem, recv_sem, partner):
        return pltpu.make_async_remote_copy(
            src_ref=source,
            dst_ref=target,
            send_sem=send_sem,
            recv_sem=recv_sem,
            device_id=partner,
            device_id_type=pl.DeviceIdType.MESH,
        )

    row = lax.broadcasted_iota(jnp.int32, (taps, 2 * taps), 0)
    column = lax.broadcasted_iota(jnp.int32, (taps, 2 * taps), 1)
    reverse = jnp.where(row + column == taps, 1.0, 0.0).astype(jnp.bfloat16)
    row = lax.broadcasted_iota(jnp.int32, (groups, groups), 0)
    column = lax.broadcasted_iota(jnp.int32, (groups, groups), 1)
    keep = jnp.broadcast_to(mask_ref[...].astype(jnp.float32), (groups, groups))
    keep = jnp.where(row == column, keep, 0.0).astype(jnp.bfloat16)
    kept = jnp.dot(
        keep, student_taps[...].astype(jnp.bfloat16), preferred_element_type=jnp.float32
    )
    base[0] = -jnp.dot(
        teacher_taps[...].astype(jnp.bfloat16), reverse, preferred_element_type=jnp.float32
    )
    base[1] = jnp.dot(kept.astype(jnp.bfloat16), reverse, preferred_element_type=jnp.float32)

    for slot, (k, block) in enumerate(order):
        ids = ids_ref[pl.ds(flipped(seq_me, k) * blocks + block, 1), :]
        weights[slot : slot + 1, :] = jnp.where(ids >= 4, repeat_weight, 1.0) * scale

    local[0].wait()
    local[1].wait()
    gated[taps : taps + tokens, :] = (key[...].astype(jnp.float32) * value[...].astype(jnp.float32)).astype(
        jnp.bfloat16
    )

    gated[taps + tokens :, :] = jnp.zeros((half, channels), jnp.bfloat16)

    @pl.when(seq_me == 0)
    def _():
        gated[0:taps, :] = jnp.zeros((taps, channels), jnp.bfloat16)


    def halo(target_seq):
        return remote(
            gated.at[pl.ds(tokens, taps)],
            gated.at[pl.ds(0, taps)],
            halo_sem.at[0],
            halo_sem.at[1],
            {"seq": target_seq, "chan": chan_me},
        )

    local[2].wait()

    def mix_chunk(chunk, slot, build):
        span = pl.ds(pl.multiple_of(chunk * lanes, lanes), lanes)
        start = own[-1]
        for index, block in enumerate(own[:-1]):
            start = jnp.where(slot == index, block, start)
        start = pl.multiple_of(start * taps, taps)
        windows = jnp.concatenate(
            [gated[pl.ds(start + side * half, 2 * taps), span] for side in range(2)], axis=1
        )
        lane_group = lax.broadcasted_iota(jnp.int32, (taps, 2 * lanes), 1) % lanes // width
        rows = [base[kind, pl.ds(chunk * per_chunk, per_chunk), :] for kind in range(2)]
        mixed = None
        for group in range(per_chunk):
            place = chunk * per_chunk + group
            if build:
                table = jnp.concatenate(
                    [
                        pltpu.roll(
                            jnp.broadcast_to(
                                rows[kind][group : group + 1, :], (half, 2 * taps)
                            ),
                            0,
                            1,
                            stride=1,
                            stride_axis=0,
                        ).astype(jnp.bfloat16)
                        for kind in range(2)
                    ],
                    axis=0,
                )
                tables[place] = table
            else:
                table = tables[place]
            product = jnp.dot(table, windows, preferred_element_type=jnp.float32)
            mixed = product if mixed is None else jnp.where(lane_group == group, product, mixed)
        for side in range(2):
            queries = query[pl.ds(start + side * half, half), span].astype(jnp.float32)
            for kind in range(2):
                mixes[slot, kind, side * half : (side + 1) * half, span] = (
                    queries
                    * mixed[
                        kind * half : (kind + 1) * half, side * lanes : (side + 1) * lanes
                    ]
                ).astype(jnp.bfloat16)

    def seq_copy(source, target, partner):
        return remote(
            mixes.at[source], mixes.at[target], seq_send.at[target], seq_recv.at[target], partner
        )

    def send_block(block):
        source = order.index((0, block))
        for k in range(1, seq_count):
            if k != 3:
                seq_copy(source, order.index((k, block)), seq_partners[k - 1]).start()

    @pl.loop(0, chunks, unroll=4)
    def _(chunk):
        mix_chunk(chunk, 0, True)

    greetings = len(always) + jnp.where(across, 1, 0) + jnp.where(inner, len(flips), 0)
    pl.semaphore_wait(barrier, greetings)

    @pl.when(seq_me + 1 < seq_count)
    def _():
        halo(seq_me + 1).start()

    send_block(own[0])
    local[3].wait()
    local[4].wait()

    def ring(item):
        return lax.rem(item, depth)

    quarter = half // parts

    def slab(offset):
        return pl.ds(pl.multiple_of(offset, 16), half)

    def strip(offset, piece):
        return pl.ds(pl.multiple_of(offset + piece * quarter, 16), quarter)

    def pair_down(item):
        return remote(
            part.at[ring(item), slab(others)],
            pair_in.at[item],
            pair_send.at[ring(item)],
            pair_recv.at[item],
            pair_partner,
        )

    def edge_down(item, piece):
        return remote(
            part.at[ring(item), strip(mine, piece)],
            edge_in.at[item, strip(0, piece)],
            edge_send.at[ring(item), piece],
            edge_recv.at[item, piece],
            edge_partner,
        )

    def middle(index, item, piece):
        source = part.at[ring(item), strip(mine, piece)]
        if index > 0:
            source = hold.at[index - 1, ring(item), strip(0, piece)]
        return remote(
            source,
            middle_in.at[index, item, strip(0, piece)],
            middle_send.at[index, ring(item), piece],
            middle_recv.at[index, item, piece],
            middle_partners[index],
        )

    def edge_up(item, piece):
        place = adjoint.at[item, strip(mine, piece)]
        return remote(
            place, place, up_send.at[ring(item), piece], up_recv.at[item, piece], edge_partner
        )

    def share(item, incoming=False):
        place = adjoint.at[item, slab(others if incoming else mine)]
        return remote(
            place, place, share_send.at[ring(item)], share_recv.at[item], pair_partner
        )

    def multiply(item):
        slot = item // cuts
        span = pl.ds(pl.multiple_of(item % cuts * cut, cut), cut)

        @pl.when(jnp.logical_and(slot >= blocks, item % cuts == 0))
        def _():
            seq_copy(slot, slot, seq_partners[0]).wait_recv()

        for index, block in enumerate(own):
            near = 1 + index % 2
            source = order.index((near, block))

            @pl.when(item == source * cuts)
            def _():
                seq_copy(source, order.index((3, block)), seq_partners[2 - near]).start()

        @pl.when(item >= depth)
        def _():
            pair_down(item - depth).wait_send()

            for piece in range(parts):

                @pl.when(inner)
                def _():
                    middle(0, item - depth, piece).wait_send()

                @pl.when(jnp.logical_not(inner))
                def _():
                    edge_down(item - depth, piece).wait_send()

        student = jnp.dot(mixes[slot, 1], student_w[:, span], preferred_element_type=jnp.float32)
        teacher = jnp.dot(mixes[slot, 0], teacher_w[:, span], preferred_element_type=jnp.float32)
        part[ring(item)] = (student + teacher).astype(jnp.bfloat16)
        pair_down(item).start()

    def held(item, piece):
        return part[ring(item), strip(mine, piece)].astype(jnp.float32)

    def arrived(buffer, item, piece):
        return buffer[item, strip(0, piece)].astype(jnp.float32)

    def fold_edge(item):
        pair_down(item).wait_recv()
        for piece in range(parts):
            total = held(item, piece) + arrived(pair_in, item, piece)
            part[ring(item), strip(mine, piece)] = total.astype(jnp.bfloat16)
            edge_down(item, piece).start()

    def fold_inner(item):
        pair_down(item).wait_recv()
        for piece in range(parts):
            edge_down(item, piece).wait_recv()
            total = held(item, piece) + arrived(pair_in, item, piece)
            total = total + arrived(edge_in, item, piece)
            part[ring(item), strip(mine, piece)] = total.astype(jnp.bfloat16)
            middle(0, item, piece).start()

    def exchange(index, item):
        for piece in range(parts):
            middle(index, item, piece).wait_recv()
            if index > 0:
                total = hold[index - 1, ring(item), strip(0, piece)].astype(jnp.float32)
            else:
                total = held(item, piece)
            total = total + middle_in[index, item, strip(0, piece)].astype(jnp.float32)
            total = total.astype(jnp.bfloat16)
            if index + 1 < len(flips):

                @pl.when(item >= depth)
                def _():
                    middle(index + 1, item - depth, piece).wait_send()

                hold[index, ring(item), strip(0, piece)] = total
                middle(index + 1, item, piece).start()
            else:

                @pl.when(item >= depth)
                def _():
                    edge_up(item - depth, piece).wait_send()

                adjoint[item, strip(mine, piece)] = total
                edge_up(item, piece).start()
        if index + 1 == len(flips):
            send_share(item)

    def send_share(item):
        @pl.when(item >= depth)
        def _():
            share(item - depth).wait_send()

        share(item).start()

    def spread_edge(item):
        for piece in range(parts):
            edge_up(item, piece).wait_recv()
        send_share(item)

    def accumulate(item):
        slot = item // cuts
        span = pl.ds(pl.multiple_of(item % cuts * cut, cut), cut)
        share(item, True).wait_recv()

        @pl.when(item % cuts == 0)
        def _():
            turned = mixes[slot, 1].T.astype(jnp.float32)
            turned = (turned * weights[pl.ds(slot, 1), :]).astype(jnp.bfloat16)

            @pl.when(slot % 2 == 0)
            def _():
                transposed[:, 0:taps] = turned

            @pl.when(slot % 2 == 1)
            def _():
                transposed[:, taps : 2 * taps] = turned

        def product():
            both = jnp.concatenate([adjoint[item - cuts], adjoint[item]], axis=0)
            return jnp.dot(transposed[...], both, preferred_element_type=jnp.float32)

        @pl.when(slot == 1)
        def _():
            total_ref[:, span] = product()

        @pl.when(jnp.logical_and(slot > 1, slot % 2 == 1))
        def _():
            total_ref[:, span] += product()

    assert chunks % cuts == 0
    per_step = chunks // cuts

    def mix_late(step):
        slot = step // cuts + 1

        @pl.when(jnp.logical_and(step == (blocks - 2) * cuts, seq_me > 0))
        def _():
            halo(seq_me).wait_recv()

        @pl.when(slot < blocks)
        def _():
            @pl.loop(0, per_step)
            def _(index):
                mix_chunk(step % cuts * per_step + index, slot, False)

        for late in range(1, blocks):

            @pl.when(step == late * cuts - 1)
            def _():
                send_block(own[late])

    last_lag = edge_lag + exchange_lag * len(flips)
    is_edge = jnp.logical_not(inner)
    stages = []
    stages += [
        (functools.partial(exchange, index), edge_lag + exchange_lag * (index + 1), inner)
        for index in range(len(flips) - 1, -1, -1)
    ]
    stages += [(fold_inner, edge_lag, inner)]
    stages += [(multiply, 0, None)]
    stages += [(fold_edge, pair_lag, is_edge)]
    stages += [(spread_edge, last_lag + up_lag, is_edge)]
    stages += [(accumulate, last_lag + share_lag + jnp.where(inner, 0, up_lag), None)]

    @pl.loop(0, items + last_lag + up_lag + share_lag)
    def _(step):
        for stage, lag, role in stages:
            item = step - lag
            active = jnp.logical_and(item >= 0, item < items)
            if role is not None:
                active = jnp.logical_and(active, role)

            @pl.when(active)
            def _():
                stage(item)

            if stage is fold_edge:
                mix_late(step)

    @pl.when(seq_me + 1 < seq_count)
    def _():
        halo(seq_me + 1).wait_send()

    for slot in range(blocks, len(order)):
        seq_copy(slot, slot, seq_partners[0]).wait_send()

    @pl.loop(items - depth, items)
    def _(item):
        pair_down(item).wait_send()
        share(item).wait_send()

        for piece in range(parts):

            @pl.when(inner)
            def _():
                for index in range(len(flips)):
                    middle(index, item, piece).wait_send()
                edge_up(item, piece).wait_send()

            @pl.when(jnp.logical_not(inner))
            def _():
                edge_down(item, piece).wait_send()


def body(
    query_stream,
    key_stream,
    value_stream,
    teacher_filter,
    student_filter,
    group_mask,
    base_ids,
    teacher_proj,
    student_proj,
):
    tokens, channels = query_stream.shape
    groups, taps = teacher_filter.shape
    width = channels // groups
    seq_count = lax.axis_size("seq")
    chan_count = lax.axis_size("chan")
    columns = teacher_proj.shape[1]
    scale = float(tokens * seq_count) ** (-0.5)
    slots = len(slot_order(seq_count, tokens // taps))
    cut = min(widest_cut, columns)
    items = slots * (columns // cut)
    flips = len(exchange_flips(chan_count))
    half = taps // 2

    any_spec = pl.BlockSpec(memory_space=pl.ANY)
    vmem_spec = pl.BlockSpec(memory_space=pltpu.VMEM)
    dma = pltpu.SemaphoreType.DMA
    bf16 = jnp.bfloat16
    return pl.pallas_call(
        functools.partial(fused_kernel, seq_count, chan_count, width, scale),
        out_shape=pltpu.VMEM((channels, columns), jnp.float32),
        in_specs=[any_spec] * 3 + [vmem_spec] * 4 + [any_spec] * 2,
        out_specs=vmem_spec,
        scratch_shapes=[
            pltpu.VMEM((tokens, channels), bf16),
            pltpu.VMEM((tokens, channels), bf16),
            pltpu.VMEM((tokens, channels), bf16),
            pltpu.VMEM((taps + tokens + half, channels), bf16),
            pltpu.VMEM((2, groups, 2 * taps), jnp.float32),
            pltpu.VMEM((groups, taps, 2 * taps), bf16),
            pltpu.VMEM((slots, taps), jnp.float32),
            pltpu.VMEM((slots, 2, taps, channels), bf16),
            pltpu.VMEM(teacher_proj.shape, bf16),
            pltpu.VMEM(student_proj.shape, bf16),
            pltpu.VMEM((depth, taps, cut), bf16),
            pltpu.VMEM((max(1, flips - 1), depth, half, cut), bf16),
            pltpu.VMEM((items, taps, cut), bf16),
            pltpu.VMEM((channels, 2 * taps), bf16),
            pltpu.VMEM((items, half, cut), bf16),
            pltpu.VMEM((items, half, cut), bf16),
            pltpu.VMEM((flips, items, half, cut), bf16),
            dma((5,)),
            dma((2,)),
            dma((slots,)),
            dma((slots,)),
            dma((depth,)),
            dma((items,)),
            dma((depth, parts)),
            dma((items, parts)),
            dma((flips, depth, parts)),
            dma((flips, items, parts)),
            dma((depth, parts)),
            dma((items, parts)),
            dma((depth,)),
            dma((items,)),
        ],
        compiler_params=pltpu.CompilerParams(
            collective_id=0, has_side_effects=True, vmem_limit_bytes=vmem_limit
        ),
        name="fused",
    )(
        query_stream,
        key_stream,
        value_stream,
        teacher_filter,
        student_filter,
        group_mask[None, :],
        base_ids.reshape(-1, taps),
        teacher_proj,
        student_proj,
    )


def solution(mesh):
    placed = (
        P("seq", "chan"),
        P("seq", "chan"),
        P("seq", "chan"),
        P("chan", None),
        P("chan", None),
        P("chan"),
        P(),
        P("chan", "seq"),
        P("chan", "seq"),
    )
    return jax.shard_map(
        body, mesh=mesh, in_specs=placed, out_specs=P("chan", "seq"), check_vma=False
    )
```

```python
import functools

import jax
import jax.numpy as jnp
from jax import lax
from jax.experimental import pallas as pl
from jax.experimental.pallas import tpu as pltpu
from jax.sharding import PartitionSpec as P

repeat_weight = 0.1
lanes = 128
widest_cut = 512
parts = 1
trail = 4
pair_lag = 1
edge_lag = 4
exchange_lag = 3
up_lag = 3
share_lag = 2
vmem_limit = 57_000_000


def flipped(position, bits):
    result = position
    step = 1
    while step <= bits:
        if bits & step:
            result = result + step - 2 * step * ((position // step) % 2)
        step *= 2
    return result


def chan_bit(position, bit):
    return (position // (1 << bit)) % 2


def exchange_flips(chan_count):
    bits = chan_count.bit_length() - 1
    assert bits >= 3 and chan_count == 1 << bits
    return [6] + [1 << bit for bit in range(3, bits)]


def drain_steps(flips):
    return edge_lag + exchange_lag * flips + up_lag + share_lag


def own_order(blocks):
    return list(range(blocks - 1, -1, -1))


def slot_order(seq_count, blocks):
    assert seq_count >= 4
    own = own_order(blocks)
    order = [(0, block) for block in own]
    for block in own:
        order += [(1, block), (2, block)]
    for k in range(3, seq_count):
        order += [(k, block) for block in own]
    return order


def fused_kernel(
    seq_count,
    chan_count,
    width,
    scale,
    query_hbm,
    key_hbm,
    value_hbm,
    teacher_taps,
    student_taps,
    mask_ref,
    ids_ref,
    teacher_hbm,
    student_hbm,
    total_ref,
    query,
    key,
    value,
    gated,
    base,
    tables,
    weights,
    mixes,
    teacher_w,
    student_w,
    part,
    hold,
    adjoint,
    transposed,
    pair_in,
    edge_in,
    middle_in,
    local_sem,
    halo_sem,
    seq_send,
    seq_recv,
    pair_send,
    pair_recv,
    edge_send,
    edge_recv,
    middle_send,
    middle_recv,
    up_send,
    up_recv,
    share_send,
    share_recv,
):
    tokens, channels = query.shape
    taps = teacher_taps.shape[1]
    groups = teacher_taps.shape[0]
    blocks = tokens // taps
    columns = teacher_w.shape[1]
    cut = part.shape[2]
    cuts = columns // cut
    half = taps // 2
    own = own_order(blocks)
    order = slot_order(seq_count, blocks)
    items = len(order) * cuts
    flips = exchange_flips(chan_count)
    depth = drain_steps(len(flips))
    per_chunk = lanes // width
    chunks = channels // lanes
    seq_me = lax.axis_index("seq")
    chan_me = lax.axis_index("chan")
    inner = chan_bit(chan_me, 1) != chan_bit(chan_me, 2)
    mine = chan_bit(chan_me, 0) * half
    others = half - mine

    def along_chan(bits):
        return {"seq": seq_me, "chan": flipped(chan_me, bits)}

    pair_partner = along_chan(1)
    edge_partner = along_chan(2)
    middle_partners = [along_chan(bits) for bits in flips]
    seq_partners = [{"seq": flipped(seq_me, k), "chan": chan_me} for k in range(1, seq_count)]
    barrier = pltpu.get_barrier_semaphore()

    def greet(partner):
        pl.semaphore_signal(
            barrier, inc=1, device_id=partner, device_id_type=pl.DeviceIdType.MESH
        )

    always = [pair_partner, edge_partner]
    always += [seq_partners[k - 1] for k in range(1, seq_count) if k != 3]
    across = jnp.logical_or(seq_me % 4 == 1, seq_me % 4 == 2)

    @pl.when(across)
    def _():
        greet(seq_partners[2])

    for partner in always:
        greet(partner)

    @pl.when(inner)
    def _():
        for partner in middle_partners:
            greet(partner)

    fore = tokens - 2 * taps
    rows = [
        (source.at[pl.ds(start, size)], target.at[pl.ds(start, size)])
        for source, target, start, size in [
            (key_hbm, key, fore, 2 * taps),
            (value_hbm, value, fore, 2 * taps),
            (query_hbm, query, tokens - taps, taps),
            (key_hbm, key, 0, fore),
            (value_hbm, value, 0, fore),
            (query_hbm, query, 0, tokens - taps),
        ]
    ]
    projections = [(teacher_hbm, teacher_w), (student_hbm, student_w)]
    rest = pl.ds(cut, columns - cut)
    local = [
        pltpu.make_async_copy(source, target, local_sem.at[index])
        for index, (source, target) in enumerate(
            rows[:3]
            + [(s.at[:, pl.ds(0, cut)], t.at[:, pl.ds(0, cut)]) for s, t in projections]
            + rows[3:]
            + [(s.at[:, rest], t.at[:, rest]) for s, t in projections]
        )
    ]
    for copy in local:
        copy.start()

    def remote(source, target, send_sem, recv_sem, partner):
        return pltpu.make_async_remote_copy(
            src_ref=source,
            dst_ref=target,
            send_sem=send_sem,
            recv_sem=recv_sem,
            device_id=partner,
            device_id_type=pl.DeviceIdType.MESH,
        )

    row = lax.broadcasted_iota(jnp.int32, (taps, 2 * taps), 0)
    column = lax.broadcasted_iota(jnp.int32, (taps, 2 * taps), 1)
    reverse = jnp.where(row + column == taps, 1.0, 0.0).astype(jnp.bfloat16)
    row = lax.broadcasted_iota(jnp.int32, (groups, groups), 0)
    column = lax.broadcasted_iota(jnp.int32, (groups, groups), 1)
    keep = jnp.broadcast_to(mask_ref[...].astype(jnp.float32), (groups, groups))
    keep = jnp.where(row == column, keep, 0.0).astype(jnp.bfloat16)
    kept = jnp.dot(
        keep, student_taps[...].astype(jnp.bfloat16), preferred_element_type=jnp.float32
    )
    base[0] = -jnp.dot(
        teacher_taps[...].astype(jnp.bfloat16), reverse, preferred_element_type=jnp.float32
    )
    base[1] = jnp.dot(kept.astype(jnp.bfloat16), reverse, preferred_element_type=jnp.float32)

    for slot, (k, block) in enumerate(order):
        ids = ids_ref[pl.ds(flipped(seq_me, k) * blocks + block, 1), :]
        weights[slot : slot + 1, :] = jnp.where(ids >= 4, repeat_weight, 1.0) * scale

    @pl.loop(0, chunks)
    def _(chunk):
        rows = [base[kind, pl.ds(chunk * per_chunk, per_chunk), :] for kind in range(2)]
        for group in range(per_chunk):
            for kind in range(2):
                row = jnp.broadcast_to(rows[kind][group : group + 1, :], (half, 2 * taps))
                tables[chunk * per_chunk + group, kind * half : (kind + 1) * half, :] = pltpu.roll(
                    row, 0, 1, stride=1, stride_axis=0
                ).astype(jnp.bfloat16)

    def gate(start, size):
        product = key[start : start + size, :].astype(jnp.float32) * value[
            start : start + size, :
        ].astype(jnp.float32)
        gated[taps + start : taps + start + size, :] = product.astype(jnp.bfloat16)

    gated[taps + tokens :, :] = jnp.zeros((half, channels), jnp.bfloat16)
    local[0].wait()
    local[1].wait()
    gate(fore, 2 * taps)

    @pl.when(seq_me == 0)
    def _():
        gated[0:taps, :] = jnp.zeros((taps, channels), jnp.bfloat16)


    def halo(target_seq):
        return remote(
            gated.at[pl.ds(tokens, taps)],
            gated.at[pl.ds(0, taps)],
            halo_sem.at[0],
            halo_sem.at[1],
            {"seq": target_seq, "chan": chan_me},
        )

    local[2].wait()

    def mix_chunk(chunk, slot):
        span = pl.ds(pl.multiple_of(chunk * lanes, lanes), lanes)
        start = own[-1]
        for index, block in enumerate(own[:-1]):
            start = jnp.where(slot == index, block, start)
        start = pl.multiple_of(start * taps, taps)
        windows = jnp.concatenate(
            [gated[pl.ds(start + side * half, 2 * taps), span] for side in range(2)], axis=1
        )
        lane_group = lax.broadcasted_iota(jnp.int32, (taps, 2 * lanes), 1) % lanes // width
        mixed = None
        for group in range(per_chunk):
            place = chunk * per_chunk + group
            table = tables[place]
            product = jnp.dot(table, windows, preferred_element_type=jnp.float32)
            mixed = product if mixed is None else jnp.where(lane_group == group, product, mixed)
        for side in range(2):
            queries = query[pl.ds(start + side * half, half), span].astype(jnp.float32)
            for kind in range(2):
                mixes[slot, kind, side * half : (side + 1) * half, span] = (
                    queries
                    * mixed[
                        kind * half : (kind + 1) * half, side * lanes : (side + 1) * lanes
                    ]
                ).astype(jnp.bfloat16)

    def seq_copy(source, target, partner):
        return remote(
            mixes.at[source], mixes.at[target], seq_send.at[target], seq_recv.at[target], partner
        )

    def send_block(block):
        source = order.index((0, block))
        for k in range(1, seq_count):
            if k != 3:
                seq_copy(source, order.index((k, block)), seq_partners[k - 1]).start()

    @pl.loop(0, chunks, unroll=8)
    def _(chunk):
        mix_chunk(chunk, 0)

    greetings = len(always) + jnp.where(across, 1, 0) + jnp.where(inner, len(flips), 0)
    pl.semaphore_wait(barrier, greetings)

    @pl.when(seq_me + 1 < seq_count)
    def _():
        halo(seq_me + 1).start()

    send_block(own[0])
    local[3].wait()
    local[4].wait()

    def ring(item):
        return lax.rem(item, depth)

    quarter = half // parts

    def slab(offset):
        return pl.ds(pl.multiple_of(offset, 16), half)

    def strip(offset, piece):
        return pl.ds(pl.multiple_of(offset + piece * quarter, 16), quarter)

    def pair_down(item):
        return remote(
            part.at[ring(item), slab(others)],
            pair_in.at[item],
            pair_send.at[ring(item)],
            pair_recv.at[item],
            pair_partner,
        )

    def edge_down(item, piece):
        return remote(
            part.at[ring(item), strip(mine, piece)],
            edge_in.at[item, strip(0, piece)],
            edge_send.at[ring(item), piece],
            edge_recv.at[item, piece],
            edge_partner,
        )

    def middle(index, item, piece):
        source = part.at[ring(item), strip(mine, piece)]
        if index > 0:
            source = hold.at[index - 1, ring(item), strip(0, piece)]
        return remote(
            source,
            middle_in.at[index, item, strip(0, piece)],
            middle_send.at[index, ring(item), piece],
            middle_recv.at[index, item, piece],
            middle_partners[index],
        )

    def edge_up(item, piece):
        place = adjoint.at[item, strip(mine, piece)]
        return remote(
            place, place, up_send.at[lax.rem(item, trail), piece], up_recv.at[item, piece], edge_partner
        )

    def share(item, incoming=False):
        place = adjoint.at[item, slab(others if incoming else mine)]
        return remote(
            place, place, share_send.at[lax.rem(item, trail)], share_recv.at[item], pair_partner
        )

    def multiply(item):
        slot = item // cuts
        span = pl.ds(pl.multiple_of(item % cuts * cut, cut), cut)

        @pl.when(jnp.logical_and(slot >= blocks, item % cuts == 0))
        def _():
            seq_copy(slot, slot, seq_partners[0]).wait_recv()

        for index, block in enumerate(own):
            near = 1 + index % 2
            source = order.index((near, block))

            @pl.when(item == source * cuts)
            def _():
                seq_copy(source, order.index((3, block)), seq_partners[2 - near]).start()

        @pl.when(item == 1)
        def _():
            for copy in local[8:]:
                copy.wait()

        student = jnp.dot(mixes[slot, 1], student_w[:, span], preferred_element_type=jnp.float32)
        teacher = jnp.dot(mixes[slot, 0], teacher_w[:, span], preferred_element_type=jnp.float32)
        part[ring(item)] = (student + teacher).astype(jnp.bfloat16)
        pair_down(item).start()

    def release(item):
        pair_down(item).wait_send()
        for piece in range(parts):

            @pl.when(inner)
            def _():
                for index in range(len(flips)):
                    middle(index, item, piece).wait_send()

            @pl.when(jnp.logical_not(inner))
            def _():
                edge_down(item, piece).wait_send()

    def held(item, piece):
        return part[ring(item), strip(mine, piece)].astype(jnp.float32)

    def arrived(buffer, item, piece):
        return buffer[item, strip(0, piece)].astype(jnp.float32)

    def fold_edge(item):
        pair_down(item).wait_recv()
        for piece in range(parts):
            total = held(item, piece) + arrived(pair_in, item, piece)
            part[ring(item), strip(mine, piece)] = total.astype(jnp.bfloat16)
            edge_down(item, piece).start()

    def fold_inner(item):
        pair_down(item).wait_recv()
        for piece in range(parts):
            edge_down(item, piece).wait_recv()
            total = held(item, piece) + arrived(pair_in, item, piece)
            total = total + arrived(edge_in, item, piece)
            part[ring(item), strip(mine, piece)] = total.astype(jnp.bfloat16)
            middle(0, item, piece).start()

    def exchange(index, item):
        for piece in range(parts):
            middle(index, item, piece).wait_recv()
            if index > 0:
                total = hold[index - 1, ring(item), strip(0, piece)].astype(jnp.float32)
            else:
                total = held(item, piece)
            total = total + middle_in[index, item, strip(0, piece)].astype(jnp.float32)
            total = total.astype(jnp.bfloat16)
            if index + 1 < len(flips):
                hold[index, ring(item), strip(0, piece)] = total
                middle(index + 1, item, piece).start()
            else:

                @pl.when(item >= trail)
                def _():
                    edge_up(item - trail, piece).wait_send()

                adjoint[item, strip(mine, piece)] = total
                edge_up(item, piece).start()
        if index + 1 == len(flips):
            send_share(item)

    def send_share(item):
        @pl.when(item >= trail)
        def _():
            share(item - trail).wait_send()

        share(item).start()

    def spread_edge(item):
        for piece in range(parts):
            edge_up(item, piece).wait_recv()
        send_share(item)

    def accumulate(item):
        slot = item // cuts
        span = pl.ds(pl.multiple_of(item % cuts * cut, cut), cut)
        share(item, True).wait_recv()

        @pl.when(item % cuts == 0)
        def _():
            turned = mixes[slot, 1].T.astype(jnp.float32)
            turned = (turned * weights[pl.ds(slot, 1), :]).astype(jnp.bfloat16)

            @pl.when(slot % 2 == 0)
            def _():
                transposed[:, 0:taps] = turned

            @pl.when(slot % 2 == 1)
            def _():
                transposed[:, taps : 2 * taps] = turned

        def product():
            both = jnp.concatenate([adjoint[item - cuts], adjoint[item]], axis=0)
            return jnp.dot(transposed[...], both, preferred_element_type=jnp.float32)

        @pl.when(slot == 1)
        def _():
            total_ref[:, span] = product()

        @pl.when(jnp.logical_and(slot > 1, slot % 2 == 1))
        def _():
            total_ref[:, span] += product()

    assert chunks % cuts == 0
    per_step = chunks // cuts

    def mix_late(step):
        slot = step // cuts + 1

        @pl.when(step == 0)
        def _():
            for copy in local[5:8]:
                copy.wait()
            gate(0, fore)

        @pl.when(jnp.logical_and(step == (blocks - 2) * cuts, seq_me > 0))
        def _():
            halo(seq_me).wait_recv()

        @pl.when(slot < blocks)
        def _():
            @pl.loop(0, per_step)
            def _(index):
                mix_chunk(step % cuts * per_step + index, slot)

        for late in range(1, blocks):

            @pl.when(step == late * cuts - 1)
            def _():
                send_block(own[late])

    last_lag = edge_lag + exchange_lag * len(flips)
    is_edge = jnp.logical_not(inner)
    stages = []
    stages += [
        (functools.partial(exchange, index), edge_lag + exchange_lag * (index + 1), inner)
        for index in range(len(flips) - 1, -1, -1)
    ]
    stages += [(fold_inner, edge_lag, inner)]
    stages += [(release, depth, None), (multiply, 0, None)]
    stages += [(fold_edge, pair_lag, is_edge)]
    stages += [(spread_edge, last_lag + up_lag, is_edge)]
    stages += [(accumulate, last_lag + share_lag + jnp.where(inner, 0, up_lag), None)]

    @pl.loop(0, items + depth)
    def _(step):
        @pl.when(step == items)
        def _():
            for slot in range(blocks, len(order)):
                seq_copy(slot, slot, seq_partners[0]).wait_send()

            @pl.when(seq_me + 1 < seq_count)
            def _():
                halo(seq_me + 1).wait_send()

        for stage, lag, role in stages:
            item = step - lag
            active = jnp.logical_and(item >= 0, item < items)
            if role is not None:
                active = jnp.logical_and(active, role)

            @pl.when(active)
            def _():
                stage(item)

            if stage is fold_edge:
                mix_late(step)

    @pl.loop(items - trail, items)
    def _(item):
        share(item).wait_send()

        @pl.when(inner)
        def _():
            for piece in range(parts):
                edge_up(item, piece).wait_send()


def body(
    query_stream,
    key_stream,
    value_stream,
    teacher_filter,
    student_filter,
    group_mask,
    base_ids,
    teacher_proj,
    student_proj,
):
    tokens, channels = query_stream.shape
    groups, taps = teacher_filter.shape
    width = channels // groups
    seq_count = lax.axis_size("seq")
    chan_count = lax.axis_size("chan")
    columns = teacher_proj.shape[1]
    scale = float(tokens * seq_count) ** (-0.5)
    slots = len(slot_order(seq_count, tokens // taps))
    cut = min(widest_cut, columns)
    items = slots * (columns // cut)
    flips = len(exchange_flips(chan_count))
    depth = drain_steps(flips)
    half = taps // 2

    any_spec = pl.BlockSpec(memory_space=pl.ANY)
    vmem_spec = pl.BlockSpec(memory_space=pltpu.VMEM)
    dma = pltpu.SemaphoreType.DMA
    bf16 = jnp.bfloat16
    return pl.pallas_call(
        functools.partial(fused_kernel, seq_count, chan_count, width, scale),
        out_shape=pltpu.VMEM((channels, columns), jnp.float32),
        in_specs=[any_spec] * 3 + [vmem_spec] * 4 + [any_spec] * 2,
        out_specs=vmem_spec,
        scratch_shapes=[
            pltpu.VMEM((tokens, channels), bf16),
            pltpu.VMEM((tokens, channels), bf16),
            pltpu.VMEM((tokens, channels), bf16),
            pltpu.VMEM((taps + tokens + half, channels), bf16),
            pltpu.VMEM((2, groups, 2 * taps), jnp.float32),
            pltpu.VMEM((groups, taps, 2 * taps), bf16),
            pltpu.VMEM((slots, taps), jnp.float32),
            pltpu.VMEM((slots, 2, taps, channels), bf16),
            pltpu.VMEM(teacher_proj.shape, bf16),
            pltpu.VMEM(student_proj.shape, bf16),
            pltpu.VMEM((depth, taps, cut), bf16),
            pltpu.VMEM((max(1, flips - 1), depth, half, cut), bf16),
            pltpu.VMEM((items, taps, cut), bf16),
            pltpu.VMEM((channels, 2 * taps), bf16),
            pltpu.VMEM((items, half, cut), bf16),
            pltpu.VMEM((items, half, cut), bf16),
            pltpu.VMEM((flips, items, half, cut), bf16),
            dma((10,)),
            dma((2,)),
            dma((slots,)),
            dma((slots,)),
            dma((depth,)),
            dma((items,)),
            dma((depth, parts)),
            dma((items, parts)),
            dma((flips, depth, parts)),
            dma((flips, items, parts)),
            dma((trail, parts)),
            dma((items, parts)),
            dma((trail,)),
            dma((items,)),
        ],
        compiler_params=pltpu.CompilerParams(
            collective_id=0, has_side_effects=True, vmem_limit_bytes=vmem_limit
        ),
        name="fused",
    )(
        query_stream,
        key_stream,
        value_stream,
        teacher_filter,
        student_filter,
        group_mask[None, :],
        base_ids.reshape(-1, taps),
        teacher_proj,
        student_proj,
    )


def solution(mesh):
    placed = (
        P("seq", "chan"),
        P("seq", "chan"),
        P("seq", "chan"),
        P("chan", None),
        P("chan", None),
        P("chan"),
        P(),
        P("chan", "seq"),
        P("chan", "seq"),
    )
    return jax.shard_map(
        body, mesh=mesh, in_specs=placed, out_specs=P("chan", "seq"), check_vma=False
    )
```

```python
import functools

import jax
import jax.numpy as jnp
from jax import lax
from jax.experimental import pallas as pl
from jax.experimental.pallas import tpu as pltpu
from jax.sharding import PartitionSpec as P

repeat_weight = 0.1
lanes = 128
widest_cut = 512
parts = 1
trail = 4
pair_lag = 1
edge_lag = 4
exchange_lag = 3
up_lag = 3
share_lag = 2
vmem_limit = 57_000_000


def flipped(position, bits):
    result = position
    step = 1
    while step <= bits:
        if bits & step:
            result = result + step - 2 * step * ((position // step) % 2)
        step *= 2
    return result


def chan_bit(position, bit):
    return (position // (1 << bit)) % 2


def exchange_flips(chan_count):
    bits = chan_count.bit_length() - 1
    assert bits >= 3 and chan_count == 1 << bits
    return [6] + [1 << bit for bit in range(3, bits)]


def drain_steps(flips):
    return edge_lag + exchange_lag * flips + up_lag + share_lag


def own_order(blocks):
    return list(range(blocks - 1, -1, -1))


def slot_order(seq_count, blocks):
    assert seq_count >= 4
    own = own_order(blocks)
    order = [(0, block) for block in own]
    for block in own:
        order += [(1, block), (2, block)]
    for k in range(3, seq_count):
        order += [(k, block) for block in own]
    return order


def fused_kernel(
    seq_count,
    chan_count,
    width,
    scale,
    query_hbm,
    key_hbm,
    value_hbm,
    teacher_taps,
    student_taps,
    mask_ref,
    ids_ref,
    teacher_hbm,
    student_hbm,
    total_ref,
    query,
    key,
    value,
    gated,
    base,
    tables,
    weights,
    mixes,
    teacher_w,
    student_w,
    part,
    hold,
    adjoint,
    transposed,
    pair_in,
    edge_in,
    middle_in,
    local_sem,
    halo_sem,
    seq_send,
    seq_recv,
    pair_send,
    pair_recv,
    edge_send,
    edge_recv,
    middle_send,
    middle_recv,
    up_send,
    up_recv,
    share_send,
    share_recv,
):
    tokens, channels = query.shape
    taps = teacher_taps.shape[1]
    groups = teacher_taps.shape[0]
    blocks = tokens // taps
    columns = teacher_w.shape[1]
    cut = part.shape[2]
    cuts = columns // cut
    half = taps // 2
    own = own_order(blocks)
    order = slot_order(seq_count, blocks)
    items = len(order) * cuts
    flips = exchange_flips(chan_count)
    depth = drain_steps(len(flips))
    per_chunk = lanes // width
    chunks = channels // lanes
    seq_me = lax.axis_index("seq")
    chan_me = lax.axis_index("chan")
    inner = chan_bit(chan_me, 1) != chan_bit(chan_me, 2)
    mine = chan_bit(chan_me, 0) * half
    others = half - mine

    def along_chan(bits):
        return {"seq": seq_me, "chan": flipped(chan_me, bits)}

    pair_partner = along_chan(1)
    edge_partner = along_chan(2)
    middle_partners = [along_chan(bits) for bits in flips]
    seq_partners = [{"seq": flipped(seq_me, k), "chan": chan_me} for k in range(1, seq_count)]
    barrier = pltpu.get_barrier_semaphore()

    def greet(partner):
        pl.semaphore_signal(
            barrier, inc=1, device_id=partner, device_id_type=pl.DeviceIdType.MESH
        )

    always = [pair_partner, edge_partner]
    always += [seq_partners[k - 1] for k in range(1, seq_count) if k != 3]
    across = jnp.logical_or(seq_me % 4 == 1, seq_me % 4 == 2)

    @pl.when(across)
    def _():
        greet(seq_partners[2])

    for partner in always:
        greet(partner)

    @pl.when(inner)
    def _():
        for partner in middle_partners:
            greet(partner)

    fore = tokens - 2 * taps
    rows = [
        (source.at[pl.ds(start, size)], target.at[pl.ds(start, size)])
        for source, target, start, size in [
            (key_hbm, key, fore, 2 * taps),
            (value_hbm, value, fore, 2 * taps),
            (query_hbm, query, tokens - taps, taps),
            (key_hbm, key, 0, fore),
            (value_hbm, value, 0, fore),
            (query_hbm, query, 0, tokens - taps),
        ]
    ]
    projections = [(teacher_hbm, teacher_w), (student_hbm, student_w)]
    rest = pl.ds(cut, columns - cut)
    local = [
        pltpu.make_async_copy(source, target, local_sem.at[index])
        for index, (source, target) in enumerate(
            rows[:3]
            + [(s.at[:, pl.ds(0, cut)], t.at[:, pl.ds(0, cut)]) for s, t in projections]
            + rows[3:]
            + [(s.at[:, rest], t.at[:, rest]) for s, t in projections]
        )
    ]
    for copy in local:
        copy.start()

    def remote(source, target, send_sem, recv_sem, partner):
        return pltpu.make_async_remote_copy(
            src_ref=source,
            dst_ref=target,
            send_sem=send_sem,
            recv_sem=recv_sem,
            device_id=partner,
            device_id_type=pl.DeviceIdType.MESH,
        )

    row = lax.broadcasted_iota(jnp.int32, (taps, 2 * taps), 0)
    column = lax.broadcasted_iota(jnp.int32, (taps, 2 * taps), 1)
    reverse = jnp.where(row + column == taps, 1.0, 0.0).astype(jnp.bfloat16)
    row = lax.broadcasted_iota(jnp.int32, (groups, groups), 0)
    column = lax.broadcasted_iota(jnp.int32, (groups, groups), 1)
    keep = jnp.broadcast_to(mask_ref[...].astype(jnp.float32), (groups, groups))
    keep = jnp.where(row == column, keep, 0.0).astype(jnp.bfloat16)
    kept = jnp.dot(
        keep, student_taps[...].astype(jnp.bfloat16), preferred_element_type=jnp.float32
    )
    base[0] = -jnp.dot(
        teacher_taps[...].astype(jnp.bfloat16), reverse, preferred_element_type=jnp.float32
    )
    base[1] = jnp.dot(kept.astype(jnp.bfloat16), reverse, preferred_element_type=jnp.float32)

    for slot, (k, block) in enumerate(order):
        ids = ids_ref[pl.ds(flipped(seq_me, k) * blocks + block, 1), :]
        weights[slot : slot + 1, :] = jnp.where(ids >= 4, repeat_weight, 1.0) * scale

    @pl.loop(0, chunks, unroll=4)
    def _(chunk):
        rows = [base[kind, pl.ds(chunk * per_chunk, per_chunk), :] for kind in range(2)]
        for group in range(per_chunk):
            for kind in range(2):
                row = jnp.broadcast_to(rows[kind][group : group + 1, :], (half, 2 * taps))
                tables[chunk * per_chunk + group, kind * half : (kind + 1) * half, :] = pltpu.roll(
                    row, 0, 1, stride=1, stride_axis=0
                ).astype(jnp.bfloat16)

    def gate(start, size):
        product = key[start : start + size, :].astype(jnp.float32) * value[
            start : start + size, :
        ].astype(jnp.float32)
        gated[taps + start : taps + start + size, :] = product.astype(jnp.bfloat16)

    gated[taps + tokens :, :] = jnp.zeros((half, channels), jnp.bfloat16)
    local[0].wait()
    local[1].wait()
    gate(fore, 2 * taps)

    @pl.when(seq_me == 0)
    def _():
        gated[0:taps, :] = jnp.zeros((taps, channels), jnp.bfloat16)


    def halo(target_seq):
        return remote(
            gated.at[pl.ds(tokens, taps)],
            gated.at[pl.ds(0, taps)],
            halo_sem.at[0],
            halo_sem.at[1],
            {"seq": target_seq, "chan": chan_me},
        )

    local[2].wait()

    def mix_chunk(chunk, slot):
        span = pl.ds(pl.multiple_of(chunk * lanes, lanes), lanes)
        start = own[-1]
        for index, block in enumerate(own[:-1]):
            start = jnp.where(slot == index, block, start)
        start = pl.multiple_of(start * taps, taps)
        windows = jnp.concatenate(
            [gated[pl.ds(start + side * half, 2 * taps), span] for side in range(2)], axis=1
        )
        lane_group = lax.broadcasted_iota(jnp.int32, (taps, 2 * lanes), 1) % lanes // width
        mixed = None
        for group in range(per_chunk):
            place = chunk * per_chunk + group
            table = tables[place]
            product = jnp.dot(table, windows, preferred_element_type=jnp.float32)
            mixed = product if mixed is None else jnp.where(lane_group == group, product, mixed)
        for side in range(2):
            queries = query[pl.ds(start + side * half, half), span].astype(jnp.float32)
            for kind in range(2):
                mixes[slot, kind, side * half : (side + 1) * half, span] = (
                    queries
                    * mixed[
                        kind * half : (kind + 1) * half, side * lanes : (side + 1) * lanes
                    ]
                ).astype(jnp.bfloat16)

    def seq_copy(source, target, partner):
        return remote(
            mixes.at[source], mixes.at[target], seq_send.at[target], seq_recv.at[target], partner
        )

    def send_block(block):
        source = order.index((0, block))
        for k in range(1, seq_count):
            if k != 3:
                seq_copy(source, order.index((k, block)), seq_partners[k - 1]).start()

    @pl.loop(0, chunks, unroll=8)
    def _(chunk):
        mix_chunk(chunk, 0)

    greetings = len(always) + jnp.where(across, 1, 0) + jnp.where(inner, len(flips), 0)
    pl.semaphore_wait(barrier, greetings)

    @pl.when(seq_me + 1 < seq_count)
    def _():
        halo(seq_me + 1).start()

    send_block(own[0])
    local[3].wait()
    local[4].wait()

    def ring(item):
        return lax.rem(item, depth)

    quarter = half // parts

    def slab(offset):
        return pl.ds(pl.multiple_of(offset, 16), half)

    def strip(offset, piece):
        return pl.ds(pl.multiple_of(offset + piece * quarter, 16), quarter)

    def pair_down(item):
        return remote(
            part.at[ring(item), slab(others)],
            pair_in.at[item],
            pair_send.at[ring(item)],
            pair_recv.at[item],
            pair_partner,
        )

    def edge_down(item, piece):
        return remote(
            part.at[ring(item), strip(mine, piece)],
            edge_in.at[item, strip(0, piece)],
            edge_send.at[ring(item), piece],
            edge_recv.at[item, piece],
            edge_partner,
        )

    def middle(index, item, piece):
        source = part.at[ring(item), strip(mine, piece)]
        if index > 0:
            source = hold.at[index - 1, ring(item), strip(0, piece)]
        return remote(
            source,
            middle_in.at[index, item, strip(0, piece)],
            middle_send.at[index, ring(item), piece],
            middle_recv.at[index, item, piece],
            middle_partners[index],
        )

    def edge_up(item, piece):
        place = adjoint.at[item, strip(mine, piece)]
        return remote(
            place, place, up_send.at[lax.rem(item, trail), piece], up_recv.at[item, piece], edge_partner
        )

    def share(item, incoming=False):
        place = adjoint.at[item, slab(others if incoming else mine)]
        return remote(
            place, place, share_send.at[lax.rem(item, trail)], share_recv.at[item], pair_partner
        )

    def multiply(item):
        slot = item // cuts
        span = pl.ds(pl.multiple_of(item % cuts * cut, cut), cut)

        @pl.when(jnp.logical_and(slot >= blocks, item % cuts == 0))
        def _():
            seq_copy(slot, slot, seq_partners[0]).wait_recv()

        for index, block in enumerate(own):
            near = 1 + index % 2
            source = order.index((near, block))

            @pl.when(item == source * cuts)
            def _():
                seq_copy(source, order.index((3, block)), seq_partners[2 - near]).start()

        @pl.when(item == 1)
        def _():
            for copy in local[8:]:
                copy.wait()

        student = jnp.dot(mixes[slot, 1], student_w[:, span], preferred_element_type=jnp.float32)
        teacher = jnp.dot(mixes[slot, 0], teacher_w[:, span], preferred_element_type=jnp.float32)
        part[ring(item)] = (student + teacher).astype(jnp.bfloat16)
        pair_down(item).start()

    def release(item):
        pair_down(item).wait_send()
        for piece in range(parts):

            @pl.when(inner)
            def _():
                for index in range(len(flips)):
                    middle(index, item, piece).wait_send()

            @pl.when(jnp.logical_not(inner))
            def _():
                edge_down(item, piece).wait_send()

    def held(item, piece):
        return part[ring(item), strip(mine, piece)].astype(jnp.float32)

    def arrived(buffer, item, piece):
        return buffer[item, strip(0, piece)].astype(jnp.float32)

    def fold_edge(item):
        pair_down(item).wait_recv()
        for piece in range(parts):
            total = held(item, piece) + arrived(pair_in, item, piece)
            part[ring(item), strip(mine, piece)] = total.astype(jnp.bfloat16)
            edge_down(item, piece).start()

    def fold_inner(item):
        pair_down(item).wait_recv()
        for piece in range(parts):
            edge_down(item, piece).wait_recv()
            total = held(item, piece) + arrived(pair_in, item, piece)
            total = total + arrived(edge_in, item, piece)
            part[ring(item), strip(mine, piece)] = total.astype(jnp.bfloat16)
            middle(0, item, piece).start()

    def exchange(index, item):
        for piece in range(parts):
            middle(index, item, piece).wait_recv()
            if index > 0:
                total = hold[index - 1, ring(item), strip(0, piece)].astype(jnp.float32)
            else:
                total = held(item, piece)
            total = total + middle_in[index, item, strip(0, piece)].astype(jnp.float32)
            total = total.astype(jnp.bfloat16)
            if index + 1 < len(flips):
                hold[index, ring(item), strip(0, piece)] = total
                middle(index + 1, item, piece).start()
            else:

                @pl.when(item >= trail)
                def _():
                    edge_up(item - trail, piece).wait_send()

                adjoint[item, strip(mine, piece)] = total
                edge_up(item, piece).start()
        if index + 1 == len(flips):
            send_share(item)

    def send_share(item):
        @pl.when(item >= trail)
        def _():
            share(item - trail).wait_send()

        share(item).start()

    def spread_edge(item):
        for piece in range(parts):
            edge_up(item, piece).wait_recv()
        send_share(item)

    def accumulate(item):
        slot = item // cuts
        span = pl.ds(pl.multiple_of(item % cuts * cut, cut), cut)
        share(item, True).wait_recv()

        @pl.when(item % cuts == 0)
        def _():
            turned = mixes[slot, 1].T.astype(jnp.float32)
            turned = (turned * weights[pl.ds(slot, 1), :]).astype(jnp.bfloat16)

            @pl.when(slot % 2 == 0)
            def _():
                transposed[:, 0:taps] = turned

            @pl.when(slot % 2 == 1)
            def _():
                transposed[:, taps : 2 * taps] = turned

        def product():
            both = jnp.concatenate([adjoint[item - cuts], adjoint[item]], axis=0)
            return jnp.dot(transposed[...], both, preferred_element_type=jnp.float32)

        @pl.when(slot == 1)
        def _():
            total_ref[:, span] = product()

        @pl.when(jnp.logical_and(slot > 1, slot % 2 == 1))
        def _():
            total_ref[:, span] += product()

    assert chunks % cuts == 0
    per_step = chunks // cuts

    def mix_late(step):
        slot = step // cuts + 1

        @pl.when(step == 0)
        def _():
            for copy in local[5:8]:
                copy.wait()
            gate(0, fore)

        @pl.when(jnp.logical_and(step == (blocks - 2) * cuts, seq_me > 0))
        def _():
            halo(seq_me).wait_recv()

        @pl.when(slot < blocks)
        def _():
            @pl.loop(0, per_step)
            def _(index):
                mix_chunk(step % cuts * per_step + index, slot)

        for late in range(1, blocks):

            @pl.when(step == late * cuts - 1)
            def _():
                send_block(own[late])

    last_lag = edge_lag + exchange_lag * len(flips)
    is_edge = jnp.logical_not(inner)
    stages = []
    stages += [
        (functools.partial(exchange, index), edge_lag + exchange_lag * (index + 1), inner)
        for index in range(len(flips) - 1, -1, -1)
    ]
    stages += [(fold_inner, edge_lag, inner)]
    stages += [(release, depth, None), (multiply, 0, None)]
    stages += [(fold_edge, pair_lag, is_edge)]
    stages += [(spread_edge, last_lag + up_lag, is_edge)]
    stages += [(accumulate, last_lag + share_lag + jnp.where(inner, 0, up_lag), None)]

    @pl.loop(0, items + depth)
    def _(step):
        @pl.when(step == items)
        def _():
            for slot in range(blocks, len(order)):
                seq_copy(slot, slot, seq_partners[0]).wait_send()

            @pl.when(seq_me + 1 < seq_count)
            def _():
                halo(seq_me + 1).wait_send()

        for stage, lag, role in stages:
            item = step - lag
            active = jnp.logical_and(item >= 0, item < items)
            if role is not None:
                active = jnp.logical_and(active, role)

            @pl.when(active)
            def _():
                stage(item)

            if stage is fold_edge:
                mix_late(step)

    @pl.loop(items - trail, items)
    def _(item):
        share(item).wait_send()

        @pl.when(inner)
        def _():
            for piece in range(parts):
                edge_up(item, piece).wait_send()


def body(
    query_stream,
    key_stream,
    value_stream,
    teacher_filter,
    student_filter,
    group_mask,
    base_ids,
    teacher_proj,
    student_proj,
):
    tokens, channels = query_stream.shape
    groups, taps = teacher_filter.shape
    width = channels // groups
    seq_count = lax.axis_size("seq")
    chan_count = lax.axis_size("chan")
    columns = teacher_proj.shape[1]
    scale = float(tokens * seq_count) ** (-0.5)
    slots = len(slot_order(seq_count, tokens // taps))
    cut = min(widest_cut, columns)
    items = slots * (columns // cut)
    flips = len(exchange_flips(chan_count))
    depth = drain_steps(flips)
    half = taps // 2

    any_spec = pl.BlockSpec(memory_space=pl.ANY)
    vmem_spec = pl.BlockSpec(memory_space=pltpu.VMEM)
    dma = pltpu.SemaphoreType.DMA
    bf16 = jnp.bfloat16
    return pl.pallas_call(
        functools.partial(fused_kernel, seq_count, chan_count, width, scale),
        out_shape=pltpu.VMEM((channels, columns), jnp.float32),
        in_specs=[any_spec] * 3 + [vmem_spec] * 4 + [any_spec] * 2,
        out_specs=vmem_spec,
        scratch_shapes=[
            pltpu.VMEM((tokens, channels), bf16),
            pltpu.VMEM((tokens, channels), bf16),
            pltpu.VMEM((tokens, channels), bf16),
            pltpu.VMEM((taps + tokens + half, channels), bf16),
            pltpu.VMEM((2, groups, 2 * taps), jnp.float32),
            pltpu.VMEM((groups, taps, 2 * taps), bf16),
            pltpu.VMEM((slots, taps), jnp.float32),
            pltpu.VMEM((slots, 2, taps, channels), bf16),
            pltpu.VMEM(teacher_proj.shape, bf16),
            pltpu.VMEM(student_proj.shape, bf16),
            pltpu.VMEM((depth, taps, cut), bf16),
            pltpu.VMEM((max(1, flips - 1), depth, half, cut), bf16),
            pltpu.VMEM((items, taps, cut), bf16),
            pltpu.VMEM((channels, 2 * taps), bf16),
            pltpu.VMEM((items, half, cut), bf16),
            pltpu.VMEM((items, half, cut), bf16),
            pltpu.VMEM((flips, items, half, cut), bf16),
            dma((10,)),
            dma((2,)),
            dma((slots,)),
            dma((slots,)),
            dma((depth,)),
            dma((items,)),
            dma((depth, parts)),
            dma((items, parts)),
            dma((flips, depth, parts)),
            dma((flips, items, parts)),
            dma((trail, parts)),
            dma((items, parts)),
            dma((trail,)),
            dma((items,)),
        ],
        compiler_params=pltpu.CompilerParams(
            collective_id=0, has_side_effects=True, vmem_limit_bytes=vmem_limit
        ),
        name="fused",
    )(
        query_stream,
        key_stream,
        value_stream,
        teacher_filter,
        student_filter,
        group_mask[None, :],
        base_ids.reshape(-1, taps),
        teacher_proj,
        student_proj,
    )


def solution(mesh):
    placed = (
        P("seq", "chan"),
        P("seq", "chan"),
        P("seq", "chan"),
        P("chan", None),
        P("chan", None),
        P("chan"),
        P(),
        P("chan", "seq"),
        P("chan", "seq"),
    )
    return jax.shard_map(
        body, mesh=mesh, in_specs=placed, out_specs=P("chan", "seq"), check_vma=False
    )
```

```python
import functools

import jax
import jax.numpy as jnp
from jax import lax
from jax.experimental import pallas as pl
from jax.experimental.pallas import tpu as pltpu
from jax.sharding import PartitionSpec as P

repeat_weight = 0.1
lanes = 128
widest_cut = 512
parts = 1
trail = 4
pair_lag = 1
edge_lag = 4
exchange_lag = 3
up_lag = 3
share_lag = 1
vmem_limit = 57_000_000


def flipped(position, bits):
    result = position
    step = 1
    while step <= bits:
        if bits & step:
            result = result + step - 2 * step * ((position // step) % 2)
        step *= 2
    return result


def chan_bit(position, bit):
    return (position // (1 << bit)) % 2


def exchange_flips(chan_count):
    bits = chan_count.bit_length() - 1
    assert bits >= 3 and chan_count == 1 << bits
    return [6] + [1 << bit for bit in range(3, bits)]


def drain_steps(flips):
    return edge_lag + exchange_lag * flips + up_lag + share_lag


def own_order(blocks):
    return list(range(blocks - 1, -1, -1))


def slot_order(seq_count, blocks):
    assert seq_count >= 4
    own = own_order(blocks)
    order = [(0, block) for block in own]
    for block in own:
        order += [(1, block), (2, block)]
    for k in range(3, seq_count):
        order += [(k, block) for block in own]
    return order


def fused_kernel(
    seq_count,
    chan_count,
    width,
    scale,
    query_hbm,
    key_hbm,
    value_hbm,
    teacher_taps,
    student_taps,
    mask_ref,
    ids_ref,
    teacher_hbm,
    student_hbm,
    total_ref,
    query,
    key,
    value,
    gated,
    base,
    tables,
    weights,
    mixes,
    teacher_w,
    student_w,
    part,
    hold,
    adjoint,
    transposed,
    pair_in,
    edge_in,
    middle_in,
    local_sem,
    halo_sem,
    seq_send,
    seq_recv,
    pair_send,
    pair_recv,
    edge_send,
    edge_recv,
    middle_send,
    middle_recv,
    up_send,
    up_recv,
    share_send,
    share_recv,
):
    tokens, channels = query.shape
    taps = teacher_taps.shape[1]
    groups = teacher_taps.shape[0]
    blocks = tokens // taps
    columns = teacher_w.shape[1]
    cut = part.shape[2]
    cuts = columns // cut
    half = taps // 2
    own = own_order(blocks)
    order = slot_order(seq_count, blocks)
    items = len(order) * cuts
    flips = exchange_flips(chan_count)
    depth = drain_steps(len(flips))
    per_chunk = lanes // width
    chunks = channels // lanes
    seq_me = lax.axis_index("seq")
    chan_me = lax.axis_index("chan")
    inner = chan_bit(chan_me, 1) != chan_bit(chan_me, 2)
    mine = chan_bit(chan_me, 0) * half
    others = half - mine

    def along_chan(bits):
        return {"seq": seq_me, "chan": flipped(chan_me, bits)}

    pair_partner = along_chan(1)
    edge_partner = along_chan(2)
    middle_partners = [along_chan(bits) for bits in flips]
    seq_partners = [{"seq": flipped(seq_me, k), "chan": chan_me} for k in range(1, seq_count)]
    barrier = pltpu.get_barrier_semaphore()

    def greet(partner):
        pl.semaphore_signal(
            barrier, inc=1, device_id=partner, device_id_type=pl.DeviceIdType.MESH
        )

    always = [pair_partner, edge_partner]
    always += [seq_partners[k - 1] for k in range(1, seq_count) if k != 3]
    across = jnp.logical_or(seq_me % 4 == 1, seq_me % 4 == 2)

    @pl.when(across)
    def _():
        greet(seq_partners[2])

    for partner in always:
        greet(partner)

    @pl.when(inner)
    def _():
        for partner in middle_partners:
            greet(partner)

    fore = tokens - 2 * taps
    rows = [
        (source.at[pl.ds(start, size)], target.at[pl.ds(start, size)])
        for source, target, start, size in [
            (key_hbm, key, fore, 2 * taps),
            (value_hbm, value, fore, 2 * taps),
            (query_hbm, query, tokens - taps, taps),
            (key_hbm, key, 0, fore),
            (value_hbm, value, 0, fore),
            (query_hbm, query, 0, tokens - taps),
        ]
    ]
    projections = [(teacher_hbm, teacher_w), (student_hbm, student_w)]
    rest = pl.ds(cut, columns - cut)
    local = [
        pltpu.make_async_copy(source, target, local_sem.at[index])
        for index, (source, target) in enumerate(
            rows[:3]
            + [(s.at[:, pl.ds(0, cut)], t.at[:, pl.ds(0, cut)]) for s, t in projections]
            + rows[3:]
            + [(s.at[:, rest], t.at[:, rest]) for s, t in projections]
        )
    ]
    for copy in local:
        copy.start()

    def remote(source, target, send_sem, recv_sem, partner):
        return pltpu.make_async_remote_copy(
            src_ref=source,
            dst_ref=target,
            send_sem=send_sem,
            recv_sem=recv_sem,
            device_id=partner,
            device_id_type=pl.DeviceIdType.MESH,
        )

    row = lax.broadcasted_iota(jnp.int32, (taps, 2 * taps), 0)
    column = lax.broadcasted_iota(jnp.int32, (taps, 2 * taps), 1)
    reverse = jnp.where(row + column == taps, 1.0, 0.0).astype(jnp.bfloat16)
    row = lax.broadcasted_iota(jnp.int32, (groups, groups), 0)
    column = lax.broadcasted_iota(jnp.int32, (groups, groups), 1)
    keep = jnp.broadcast_to(mask_ref[...].astype(jnp.float32), (groups, groups))
    keep = jnp.where(row == column, keep, 0.0).astype(jnp.bfloat16)
    kept = jnp.dot(
        keep, student_taps[...].astype(jnp.bfloat16), preferred_element_type=jnp.float32
    )
    base[0] = -jnp.dot(
        teacher_taps[...].astype(jnp.bfloat16), reverse, preferred_element_type=jnp.float32
    )
    base[1] = jnp.dot(kept.astype(jnp.bfloat16), reverse, preferred_element_type=jnp.float32)

    for slot, (k, block) in enumerate(order):
        ids = ids_ref[pl.ds(flipped(seq_me, k) * blocks + block, 1), :]
        weights[slot : slot + 1, :] = jnp.where(ids >= 4, repeat_weight, 1.0) * scale

    @pl.loop(0, chunks, unroll=4)
    def _(chunk):
        rows = [base[kind, pl.ds(chunk * per_chunk, per_chunk), :] for kind in range(2)]
        for group in range(per_chunk):
            for kind in range(2):
                row = jnp.broadcast_to(rows[kind][group : group + 1, :], (half, 2 * taps))
                tables[chunk * per_chunk + group, kind * half : (kind + 1) * half, :] = pltpu.roll(
                    row, 0, 1, stride=1, stride_axis=0
                ).astype(jnp.bfloat16)

    def gate(start, size):
        product = key[start : start + size, :].astype(jnp.float32) * value[
            start : start + size, :
        ].astype(jnp.float32)
        gated[taps + start : taps + start + size, :] = product.astype(jnp.bfloat16)

    gated[taps + tokens :, :] = jnp.zeros((half, channels), jnp.bfloat16)
    local[0].wait()
    local[1].wait()
    gate(fore, 2 * taps)

    @pl.when(seq_me == 0)
    def _():
        gated[0:taps, :] = jnp.zeros((taps, channels), jnp.bfloat16)


    def halo(target_seq):
        return remote(
            gated.at[pl.ds(tokens, taps)],
            gated.at[pl.ds(0, taps)],
            halo_sem.at[0],
            halo_sem.at[1],
            {"seq": target_seq, "chan": chan_me},
        )

    local[2].wait()

    def mix_chunk(chunk, slot):
        span = pl.ds(pl.multiple_of(chunk * lanes, lanes), lanes)
        start = own[-1]
        for index, block in enumerate(own[:-1]):
            start = jnp.where(slot == index, block, start)
        start = pl.multiple_of(start * taps, taps)
        windows = jnp.concatenate(
            [gated[pl.ds(start + side * half, 2 * taps), span] for side in range(2)], axis=1
        )
        lane_group = lax.broadcasted_iota(jnp.int32, (taps, 2 * lanes), 1) % lanes // width
        mixed = None
        for group in range(per_chunk):
            place = chunk * per_chunk + group
            table = tables[place]
            product = jnp.dot(table, windows, preferred_element_type=jnp.float32)
            mixed = product if mixed is None else jnp.where(lane_group == group, product, mixed)
        for side in range(2):
            queries = query[pl.ds(start + side * half, half), span].astype(jnp.float32)
            for kind in range(2):
                mixes[slot, kind, side * half : (side + 1) * half, span] = (
                    queries
                    * mixed[
                        kind * half : (kind + 1) * half, side * lanes : (side + 1) * lanes
                    ]
                ).astype(jnp.bfloat16)

    def seq_copy(source, target, partner):
        return remote(
            mixes.at[source], mixes.at[target], seq_send.at[target], seq_recv.at[target], partner
        )

    def send_block(block):
        source = order.index((0, block))
        for k in range(1, seq_count):
            if k != 3:
                seq_copy(source, order.index((k, block)), seq_partners[k - 1]).start()

    @pl.loop(0, chunks, unroll=8)
    def _(chunk):
        mix_chunk(chunk, 0)

    greetings = len(always) + jnp.where(across, 1, 0) + jnp.where(inner, len(flips), 0)
    pl.semaphore_wait(barrier, greetings)

    @pl.when(seq_me + 1 < seq_count)
    def _():
        halo(seq_me + 1).start()

    send_block(own[0])
    local[3].wait()
    local[4].wait()

    def ring(item):
        return lax.rem(item, depth)

    quarter = half // parts

    def slab(offset):
        return pl.ds(pl.multiple_of(offset, 16), half)

    def strip(offset, piece):
        return pl.ds(pl.multiple_of(offset + piece * quarter, 16), quarter)

    def pair_down(item):
        return remote(
            part.at[ring(item), slab(others)],
            pair_in.at[item],
            pair_send.at[ring(item)],
            pair_recv.at[item],
            pair_partner,
        )

    def edge_down(item, piece):
        return remote(
            part.at[ring(item), strip(mine, piece)],
            edge_in.at[item, strip(0, piece)],
            edge_send.at[ring(item), piece],
            edge_recv.at[item, piece],
            edge_partner,
        )

    def middle(index, item, piece):
        source = part.at[ring(item), strip(mine, piece)]
        if index > 0:
            source = hold.at[index - 1, ring(item), strip(0, piece)]
        return remote(
            source,
            middle_in.at[index, item, strip(0, piece)],
            middle_send.at[index, ring(item), piece],
            middle_recv.at[index, item, piece],
            middle_partners[index],
        )

    def edge_up(item, piece):
        place = adjoint.at[item, strip(mine, piece)]
        return remote(
            place, place, up_send.at[lax.rem(item, trail), piece], up_recv.at[item, piece], edge_partner
        )

    def share(item, incoming=False):
        place = adjoint.at[item, slab(others if incoming else mine)]
        return remote(
            place, place, share_send.at[lax.rem(item, trail)], share_recv.at[item], pair_partner
        )

    def multiply(item):
        slot = item // cuts
        span = pl.ds(pl.multiple_of(item % cuts * cut, cut), cut)

        @pl.when(jnp.logical_and(slot >= blocks, item % cuts == 0))
        def _():
            seq_copy(slot, slot, seq_partners[0]).wait_recv()

        for index, block in enumerate(own):
            near = 1 + index % 2
            source = order.index((near, block))

            @pl.when(item == source * cuts)
            def _():
                seq_copy(source, order.index((3, block)), seq_partners[2 - near]).start()

        @pl.when(item == 1)
        def _():
            for copy in local[8:]:
                copy.wait()

        student = jnp.dot(mixes[slot, 1], student_w[:, span], preferred_element_type=jnp.float32)
        teacher = jnp.dot(mixes[slot, 0], teacher_w[:, span], preferred_element_type=jnp.float32)
        part[ring(item)] = (student + teacher).astype(jnp.bfloat16)
        pair_down(item).start()

    def release(item):
        pair_down(item).wait_send()
        for piece in range(parts):

            @pl.when(inner)
            def _():
                for index in range(len(flips)):
                    middle(index, item, piece).wait_send()

            @pl.when(jnp.logical_not(inner))
            def _():
                edge_down(item, piece).wait_send()

    def held(item, piece):
        return part[ring(item), strip(mine, piece)].astype(jnp.float32)

    def arrived(buffer, item, piece):
        return buffer[item, strip(0, piece)].astype(jnp.float32)

    def fold_edge(item):
        pair_down(item).wait_recv()
        for piece in range(parts):
            total = held(item, piece) + arrived(pair_in, item, piece)
            part[ring(item), strip(mine, piece)] = total.astype(jnp.bfloat16)
            edge_down(item, piece).start()

    def fold_inner(item):
        pair_down(item).wait_recv()
        for piece in range(parts):
            edge_down(item, piece).wait_recv()
            total = held(item, piece) + arrived(pair_in, item, piece)
            total = total + arrived(edge_in, item, piece)
            part[ring(item), strip(mine, piece)] = total.astype(jnp.bfloat16)
            middle(0, item, piece).start()

    def exchange(index, item):
        for piece in range(parts):
            middle(index, item, piece).wait_recv()
            if index > 0:
                total = hold[index - 1, ring(item), strip(0, piece)].astype(jnp.float32)
            else:
                total = held(item, piece)
            total = total + middle_in[index, item, strip(0, piece)].astype(jnp.float32)
            total = total.astype(jnp.bfloat16)
            if index + 1 < len(flips):
                hold[index, ring(item), strip(0, piece)] = total
                middle(index + 1, item, piece).start()
            else:

                @pl.when(item >= trail)
                def _():
                    edge_up(item - trail, piece).wait_send()

                adjoint[item, strip(mine, piece)] = total
                edge_up(item, piece).start()
        if index + 1 == len(flips):
            send_share(item)

    def send_share(item):
        @pl.when(item >= trail)
        def _():
            share(item - trail).wait_send()

        share(item).start()

    def spread_edge(item):
        for piece in range(parts):
            edge_up(item, piece).wait_recv()
        send_share(item)

    def accumulate(item):
        slot = item // cuts
        span = pl.ds(pl.multiple_of(item % cuts * cut, cut), cut)
        share(item, True).wait_recv()

        @pl.when(item % cuts == 0)
        def _():
            turned = mixes[slot, 1].T.astype(jnp.float32)
            turned = (turned * weights[pl.ds(slot, 1), :]).astype(jnp.bfloat16)

            @pl.when(slot % 2 == 0)
            def _():
                transposed[:, 0:taps] = turned

            @pl.when(slot % 2 == 1)
            def _():
                transposed[:, taps : 2 * taps] = turned

        def product():
            both = jnp.concatenate([adjoint[item - cuts], adjoint[item]], axis=0)
            return jnp.dot(transposed[...], both, preferred_element_type=jnp.float32)

        @pl.when(slot == 1)
        def _():
            total_ref[:, span] = product()

        @pl.when(jnp.logical_and(slot > 1, slot % 2 == 1))
        def _():
            total_ref[:, span] += product()

    assert chunks % cuts == 0
    per_step = chunks // cuts

    def mix_late(step):
        slot = step // cuts + 1

        @pl.when(step == 0)
        def _():
            for copy in local[5:8]:
                copy.wait()
            gate(0, fore)

        @pl.when(jnp.logical_and(step == (blocks - 2) * cuts, seq_me > 0))
        def _():
            halo(seq_me).wait_recv()

        @pl.when(slot < blocks)
        def _():
            @pl.loop(0, per_step)
            def _(index):
                mix_chunk(step % cuts * per_step + index, slot)

        for late in range(1, blocks):

            @pl.when(step == late * cuts - 1)
            def _():
                send_block(own[late])

    last_lag = edge_lag + exchange_lag * len(flips)
    is_edge = jnp.logical_not(inner)
    stages = []
    stages += [
        (functools.partial(exchange, index), edge_lag + exchange_lag * (index + 1), inner)
        for index in range(len(flips) - 1, -1, -1)
    ]
    stages += [(fold_inner, edge_lag, inner)]
    stages += [(release, depth, None), (multiply, 0, None)]
    stages += [(fold_edge, pair_lag, is_edge)]
    stages += [(spread_edge, last_lag + up_lag, is_edge)]
    stages += [(accumulate, last_lag + share_lag + jnp.where(inner, 0, up_lag), None)]

    @pl.loop(0, items + depth)
    def _(step):
        @pl.when(step == items)
        def _():
            for slot in range(blocks, len(order)):
                seq_copy(slot, slot, seq_partners[0]).wait_send()

            @pl.when(seq_me + 1 < seq_count)
            def _():
                halo(seq_me + 1).wait_send()

        for stage, lag, role in stages:
            item = step - lag
            active = jnp.logical_and(item >= 0, item < items)
            if role is not None:
                active = jnp.logical_and(active, role)

            @pl.when(active)
            def _():
                stage(item)

            if stage is fold_edge:
                mix_late(step)

    @pl.loop(items - trail, items)
    def _(item):
        share(item).wait_send()

        @pl.when(inner)
        def _():
            for piece in range(parts):
                edge_up(item, piece).wait_send()


def body(
    query_stream,
    key_stream,
    value_stream,
    teacher_filter,
    student_filter,
    group_mask,
    base_ids,
    teacher_proj,
    student_proj,
):
    tokens, channels = query_stream.shape
    groups, taps = teacher_filter.shape
    width = channels // groups
    seq_count = lax.axis_size("seq")
    chan_count = lax.axis_size("chan")
    columns = teacher_proj.shape[1]
    scale = float(tokens * seq_count) ** (-0.5)
    slots = len(slot_order(seq_count, tokens // taps))
    cut = min(widest_cut, columns)
    items = slots * (columns // cut)
    flips = len(exchange_flips(chan_count))
    depth = drain_steps(flips)
    half = taps // 2

    any_spec = pl.BlockSpec(memory_space=pl.ANY)
    vmem_spec = pl.BlockSpec(memory_space=pltpu.VMEM)
    dma = pltpu.SemaphoreType.DMA
    bf16 = jnp.bfloat16
    return pl.pallas_call(
        functools.partial(fused_kernel, seq_count, chan_count, width, scale),
        out_shape=pltpu.VMEM((channels, columns), jnp.float32),
        in_specs=[any_spec] * 3 + [vmem_spec] * 4 + [any_spec] * 2,
        out_specs=vmem_spec,
        scratch_shapes=[
            pltpu.VMEM((tokens, channels), bf16),
            pltpu.VMEM((tokens, channels), bf16),
            pltpu.VMEM((tokens, channels), bf16),
            pltpu.VMEM((taps + tokens + half, channels), bf16),
            pltpu.VMEM((2, groups, 2 * taps), jnp.float32),
            pltpu.VMEM((groups, taps, 2 * taps), bf16),
            pltpu.VMEM((slots, taps), jnp.float32),
            pltpu.VMEM((slots, 2, taps, channels), bf16),
            pltpu.VMEM(teacher_proj.shape, bf16),
            pltpu.VMEM(student_proj.shape, bf16),
            pltpu.VMEM((depth, taps, cut), bf16),
            pltpu.VMEM((max(1, flips - 1), depth, half, cut), bf16),
            pltpu.VMEM((items, taps, cut), bf16),
            pltpu.VMEM((channels, 2 * taps), bf16),
            pltpu.VMEM((items, half, cut), bf16),
            pltpu.VMEM((items, half, cut), bf16),
            pltpu.VMEM((flips, items, half, cut), bf16),
            dma((10,)),
            dma((2,)),
            dma((slots,)),
            dma((slots,)),
            dma((depth,)),
            dma((items,)),
            dma((depth, parts)),
            dma((items, parts)),
            dma((flips, depth, parts)),
            dma((flips, items, parts)),
            dma((trail, parts)),
            dma((items, parts)),
            dma((trail,)),
            dma((items,)),
        ],
        compiler_params=pltpu.CompilerParams(
            collective_id=0, has_side_effects=True, vmem_limit_bytes=vmem_limit
        ),
        name="fused",
    )(
        query_stream,
        key_stream,
        value_stream,
        teacher_filter,
        student_filter,
        group_mask[None, :],
        base_ids.reshape(-1, taps),
        teacher_proj,
        student_proj,
    )


def solution(mesh):
    placed = (
        P("seq", "chan"),
        P("seq", "chan"),
        P("seq", "chan"),
        P("chan", None),
        P("chan", None),
        P("chan"),
        P(),
        P("chan", "seq"),
        P("chan", "seq"),
    )
    return jax.shard_map(
        body, mesh=mesh, in_specs=placed, out_specs=P("chan", "seq"), check_vma=False
    )
```
